32 devices in a mesh: dp: 8 (over z, core), seq: 4 (over y, x).
Axes of the slice: x: 2, y: 2, z: 4, core: 2. Of those that a mesh axis runs over, the one named last changes fastest.
Arguments:
- enc_final: bfloat16 [8, 96, 4096], P('dp', 'seq'), may hold values from -6 to 6
- norm_gain: float32 [4096], replicated, may hold values from 0.1 to 1.9
- dec_queries: bfloat16 [2, 8, 512, 2048], P(None, 'dp', 'seq'), may hold values from -48 to 48
- out_grad: bfloat16 [2, 8, 512, 2048], P(None, 'dp', 'seq'), may hold values from -6 to 6
- enc_keys: bfloat16 [2, 8, 96, 2048], P(None, 'dp', 'seq'), may hold values from -6 to 6
- enc_values: bfloat16 [2, 8, 96, 2048], P(None, 'dp', 'seq'), may hold values from -6 to 6
- key_weight: bfloat16 [2, 4096, 2048], P(None, None, 'seq'), may hold values from -0.09375 to 0.09375
- value_weight: bfloat16 [2, 4096, 2048], P(None, None, 'seq'), may hold values from -0.09375 to 0.09375
Outputs:
- enc_grad: bfloat16 [8, 96, 4096], P('dp', 'seq')
- gain_grad: float32 [4096], replicated
The draws below stay inside these ranges and needn't reach their ends.
All inputs are finite; a program needn't handle non-finite values.
Results may differ from the reference program's by a relative error of at most 0.007.
Values may be sent and summed in bfloat16 or wider, within the bound.
No kernel may reach another device: no remote copies, remote signals or barrier semaphores. Data moves between devices by JAX's collectives and lax.ppermute only.
A program may use at most 128 MiB of HBM per device.

```python
import jax
import jax.numpy as jnp
from jax import lax

D = 4096
HEADS = 32
HEAD_DIM = 64
LAYERS = 2
HD = 2048
DOCS = 8
ENC = 96
DEC = 512


def shared_keys(key):
    base = jax.random.normal(jax.random.fold_in(key, 101), (LAYERS, DOCS, ENC, HD), jnp.float32)
    return jnp.clip(base, -6.0, 6.0)


def draw_enc_keys(key, part):
    return shared_keys(key).astype(jnp.bfloat16)


def draw_dec_queries(key, part):
    drawn = 0.125 * jax.random.normal(jax.random.fold_in(key, 103), (LAYERS, DOCS, DEC, HD), jnp.float32)
    drawn = jnp.clip(drawn, -0.75, 0.75)
    return drawn.astype(jnp.bfloat16)


def level_of(stream_key, extent, split, smallest, largest):
    def one(position, blocks):
        draws = jax.random.uniform(jax.random.fold_in(jax.random.fold_in(stream_key, 6), position), (blocks,), jnp.float32, smallest / len(split), largest / len(split))
        return jnp.repeat(jnp.exp(draws), extent[position] // blocks).reshape((-1,) + (1,) * (len(extent) - position - 1))

    factor_of = one(*split[0])
    for cut in split[1:]:
        factor_of = factor_of * one(*cut)
    return factor_of


def normal_values(stream_key, shape, spread, reach, pieces=(), dtype=jnp.bfloat16):
    values = spread * jax.random.normal(stream_key, shape, jnp.float32)
    if pieces:
        values = values * level_of(stream_key, shape, pieces, -0.22, 0.18)
    return jnp.clip(values, -reach, reach).astype(dtype)


def setup_inputs(seed: int = 0) -> dict:
    key_list = jax.random.split(jax.random.key(seed), 9)
    return {
        "enc_final": normal_values(key_list[0], (DOCS, ENC, D), 1.0, 6.0, ((0, 8), (1, 4))),
        "norm_gain": jnp.clip(1.0 + 0.18 * jax.random.normal(key_list[1], (D,), jnp.float32), 0.1, 1.9),
        "dec_queries": draw_dec_queries(jax.random.fold_in(key_list[8], 71), 0),
        "out_grad": normal_values(key_list[3], (LAYERS, DOCS, DEC, HD), 1.0, 6.0, ((1, 8), (2, 4))),
        "enc_keys": draw_enc_keys(jax.random.fold_in(key_list[8], 71), 0),
        "enc_values": normal_values(key_list[5], (LAYERS, DOCS, ENC, HD), 1.0, 6.0, ((1, 8), (2, 4))),
        "key_weight": normal_values(key_list[6], (LAYERS, D, HD), D ** -0.5, 0.09375, ((2, 4),)),
        "value_weight": normal_values(key_list[7], (LAYERS, D, HD), D ** -0.5, 0.09375, ((2, 4),)),
    }


def attention_grads(query_rows, grad_rows, key_rows, value_rows):
    dec_count = query_rows.shape[0]
    enc_count = key_rows.shape[0]
    query_heads = query_rows.astype(jnp.float32).reshape(dec_count, HEADS, HEAD_DIM)
    grad_heads = grad_rows.astype(jnp.float32).reshape(dec_count, HEADS, HEAD_DIM)
    key_heads = key_rows.astype(jnp.float32).reshape(enc_count, HEADS, HEAD_DIM)
    value_heads = value_rows.astype(jnp.float32).reshape(enc_count, HEADS, HEAD_DIM)
    scores = jnp.einsum('qhd,khd->hqk', query_heads, key_heads)
    row_peak = lax.optimization_barrier(jnp.max(scores, axis=-1, keepdims=True))
    shifted = jnp.exp(scores - row_peak)
    weights = shifted / lax.optimization_barrier(jnp.sum(shifted, axis=-1, keepdims=True))
    weights_low = weights.astype(jnp.bfloat16).astype(jnp.float32)
    prob_grad = jnp.einsum('qhd,khd->hqk', grad_heads, value_heads)
    row_delta = lax.optimization_barrier(jnp.sum(weights * prob_grad, axis=-1, keepdims=True))
    score_grad = (weights * (prob_grad - row_delta)).astype(jnp.bfloat16).astype(jnp.float32)
    value_grad = jnp.einsum('hqk,qhd->khd', weights_low, grad_heads).reshape(enc_count, HEADS * HEAD_DIM)
    key_grad = jnp.einsum('hqk,qhd->khd', score_grad, query_heads).reshape(enc_count, HEADS * HEAD_DIM)
    return (key_grad.astype(jnp.bfloat16), value_grad.astype(jnp.bfloat16))

def reference(enc_final, norm_gain, dec_queries, out_grad, enc_keys, enc_values, key_weight, value_weight):

    def one_document(inputs):
        final_rows, query_all, grad_all, key_all, value_all = inputs
        state_grad = jnp.zeros((final_rows.shape[0], final_rows.shape[1]), jnp.float32)
        for layer_index in range(LAYERS):
            key_grad, value_grad = attention_grads(query_all[layer_index], grad_all[layer_index], key_all[layer_index], value_all[layer_index])
            state_grad = state_grad + jnp.dot(key_grad, key_weight[layer_index].T, preferred_element_type=jnp.float32)
            state_grad = state_grad + jnp.dot(value_grad, value_weight[layer_index].T, preferred_element_type=jnp.float32)
        final_float = final_rows.astype(jnp.float32)
        inv_rms = lax.rsqrt(lax.optimization_barrier(jnp.mean(final_float * final_float, axis=-1, keepdims=True)) + 1e-06)
        normed = final_float * inv_rms
        scaled = norm_gain[None, :] * state_grad
        grad_rows = inv_rms * (scaled - normed * lax.optimization_barrier(jnp.mean(scaled * normed, axis=-1, keepdims=True)))
        gain_term = lax.optimization_barrier(jnp.sum(state_grad * normed, axis=0))
        return (grad_rows.astype(jnp.bfloat16), gain_term)
    inputs = (enc_final, jnp.moveaxis(dec_queries, 1, 0), jnp.moveaxis(out_grad, 1, 0), jnp.moveaxis(enc_keys, 1, 0), jnp.moveaxis(enc_values, 1, 0))
    enc_grad, gain_terms = lax.map(one_document, inputs)
    gain_grad = lax.optimization_barrier(jnp.sum(gain_terms, axis=0)) / DOCS
    return (enc_grad, gain_grad)
```

```python
import functools

import jax
import jax.numpy as jnp
from jax import lax
from jax.experimental import pallas as pl
from jax.experimental.pallas import tpu as pltpu
from jax.sharding import PartitionSpec as P

HEAD_DIM = 64
LANES = 128
PROJ_BLOCK = 1024
ATTN_ROWS = 512
F32 = jnp.float32
BF16 = jnp.bfloat16


def xor_pairs(size, step):
    return [(i, i ^ step) for i in range(size)]


def pack_layer(layer, arrays, seq_size):
    rows = [a.shape[2] for a in arrays]
    cols = arrays[0].shape[3] // seq_size
    total = sum(rows)

    def kernel(q_ref, g_ref, k_ref, v_ref, *rest):
        outs, sems = rest[:seq_size], rest[seq_size]
        me = lax.axis_index("seq")
        copies = []
        for j in list(range(1, seq_size)) + [0]:
            start = pl.multiple_of((me ^ j) * cols, LANES)
            base = 0
            for i, ref in enumerate((q_ref, g_ref, k_ref, v_ref)):
                copies.append(
                    pltpu.make_async_copy(
                        ref.at[layer, 0, :, pl.ds(start, cols)],
                        outs[j].at[pl.ds(base, rows[i]), :],
                        sems.at[j, i],
                    )
                )
                base += rows[i]
        for c in copies:
            c.start()
        for c in copies:
            c.wait()

    return pl.pallas_call(
        kernel,
        out_shape=[jax.ShapeDtypeStruct((total, cols), BF16)] * seq_size,
        in_specs=[pl.BlockSpec(memory_space=pl.ANY)] * 4,
        out_specs=[pl.BlockSpec(memory_space=pl.ANY)] * seq_size,
        scratch_shapes=[pltpu.SemaphoreType.DMA((seq_size, 4))],
        name=f"pack_{layer}",
    )(*arrays)


def attention_into(bufs, dec, enc, kv_ref):
    cols = bufs[0].shape[1]
    count = len(bufs)
    per = LANES // HEAD_DIM
    group = max(1, ATTN_ROWS // dec)
    lane_head = lax.broadcasted_iota(jnp.int32, (1, LANES), 1) // HEAD_DIM
    rows = enc * count

    def stacked(base, ls):
        whole = jnp.concatenate([b[base : base + enc, ls].astype(F32) for b in bufs], axis=0)
        parts = [jnp.where(lane_head == h, whole, 0.0) for h in range(per)]
        return jnp.concatenate(parts, axis=0).astype(BF16)

    def chosen(stack):
        out = stack[:rows]
        for h in range(1, per):
            out = jnp.where(lane_head == h, stack[h * rows : (h + 1) * rows], out)
        return out.astype(BF16)

    nt = (((1,), (1,)), ((), ()))
    nn = (((1,), (0,)), ((), ()))
    for p in range(cols // LANES):
        ls = slice(p * LANES, (p + 1) * LANES)
        keys = stacked(2 * dec, ls)
        values = stacked(2 * dec + enc, ls)
        key_sum = value_sum = None
        for first in range(0, count, group):
            some = bufs[first : first + group]
            q = jnp.concatenate([b[0:dec, ls] for b in some], axis=0)
            g = jnp.concatenate([b[dec : 2 * dec, ls] for b in some], axis=0)
            width = q.shape[0]
            s = lax.dot_general(keys, q, nt, preferred_element_type=F32).reshape(per, rows, width)
            d = lax.dot_general(values, g, nt, preferred_element_type=F32).reshape(per, rows, width)
            e = jnp.exp(s - jnp.max(s, axis=1, keepdims=True))
            w = e * (1.0 / jnp.sum(e, axis=1, keepdims=True))
            delta = jnp.sum(w * d, axis=1, keepdims=True)
            ds = (w * (d - delta)).astype(BF16).reshape(per * rows, width)
            wl = w.astype(BF16).reshape(per * rows, width)
            vg = lax.dot_general(wl, g, nn, preferred_element_type=F32)
            kg = lax.dot_general(ds, q, nn, preferred_element_type=F32)
            key_sum = kg if key_sum is None else key_sum + kg
            value_sum = vg if value_sum is None else value_sum + vg
        kv_ref[:, ls] = chosen(key_sum)
        kv_ref[:, cols + p * LANES : cols + (p + 1) * LANES] = chosen(value_sum)


def layer_terms(layer, bufs, key_weight, value_weight, prior, dec, enc, last):
    count = len(bufs)
    width, cols = key_weight.shape[1], key_weight.shape[2]
    rows = enc * count
    block = PROJ_BLOCK
    nblocks = width // block

    def kernel(*refs):
        buf_refs = refs[:count]
        kw, vw = refs[count : count + 2]
        pos = count + 2
        if prior is not None:
            prior_ref = refs[pos]
            pos += 1
        n_out = count if last else 1
        outs = refs[pos : pos + n_out]
        pos += n_out
        w_ref, kv_ref, sems = refs[pos : pos + 3]
        copies = []
        for b in range(nblocks):
            pair = []
            for i, src in enumerate((kw, vw)):
                pair.append(
                    pltpu.make_async_copy(
                        src.at[layer, pl.ds(b * block, block), :],
                        w_ref.at[i, pl.ds(b * block, block), :],
                        sems.at[b, i],
                    )
                )
            copies.append(pair)
        for pair in copies:
            for c in pair:
                c.start()
        attention_into([r for r in buf_refs], dec, enc, kv_ref)
        nt = (((1,), (1,)), ((), ()))
        for b in range(nblocks):
            for c in copies[b]:
                c.wait()
            bs = slice(b * block, (b + 1) * block)
            acc = lax.dot_general(kv_ref[:, :cols], w_ref[0, bs, :], nt, preferred_element_type=F32)
            acc += lax.dot_general(kv_ref[:, cols:], w_ref[1, bs, :], nt, preferred_element_type=F32)
            if prior is not None:
                acc += prior_ref[:, bs]
            if last:
                for j in range(count):
                    piece = acc[j * enc : (j + 1) * enc]
                    outs[j][:, bs] = piece.astype(outs[j].dtype)
            else:
                outs[0][:, bs] = acc

    if last:
        out_shape = [jax.ShapeDtypeStruct((enc, width), F32 if j == 0 else BF16) for j in range(count)]
    else:
        out_shape = [jax.ShapeDtypeStruct((rows, width), F32)]
    vmem = pl.BlockSpec(memory_space=pltpu.VMEM)
    hbm = pl.BlockSpec(memory_space=pl.ANY)
    operands = list(bufs) + [key_weight, value_weight] + ([] if prior is None else [prior])
    return pl.pallas_call(
        kernel,
        out_shape=out_shape,
        in_specs=[vmem] * count + [hbm] * 2 + ([] if prior is None else [vmem]),
        out_specs=[vmem] * len(out_shape),
        scratch_shapes=[
            pltpu.VMEM((2, width, cols), BF16),
            pltpu.VMEM((rows, 2 * cols), BF16),
            pltpu.SemaphoreType.DMA((nblocks, 2)),
        ],
        name=f"layer_{layer}",
    )(*operands)


def finish(own, received, enc_final, norm_gain):
    enc, width = own.shape

    def kernel(own_ref, *refs):
        recv_refs = refs[: len(received)]
        final_ref, gain_ref, grad_ref, term_ref = refs[len(received) :]
        state = own_ref[...]
        for r in recv_refs:
            state = state + r[...].astype(F32)
        final = final_ref[0].astype(F32)
        inv_rms = lax.rsqrt(jnp.mean(final * final, axis=-1, keepdims=True) + 1e-06)
        normed = final * inv_rms
        scaled = gain_ref[...] * state
        mean = jnp.mean(scaled * normed, axis=-1, keepdims=True)
        grad_ref[0] = (inv_rms * (scaled - normed * mean)).astype(BF16)
        term_ref[...] = jnp.sum(state * normed, axis=0, keepdims=True)

    return pl.pallas_call(
        kernel,
        out_shape=[
            jax.ShapeDtypeStruct((1, enc, width), BF16),
            jax.ShapeDtypeStruct((1, width), F32),
        ],
        name="finish",
    )(own, *received, enc_final, norm_gain.reshape(1, width))


def body(
    enc_final, norm_gain, dec_queries, out_grad, enc_keys, enc_values, key_weight, value_weight
):
    seq = lax.axis_size("seq")
    docs = lax.axis_size("dp")
    layers = dec_queries.shape[0]
    dec, enc = dec_queries.shape[2], enc_keys.shape[2]
    arrays = (dec_queries, out_grad, enc_keys, enc_values)
    gathered = []
    for layer in range(layers):
        bufs = pack_layer(layer, arrays, seq)
        gathered.append(
            [bufs[0]] + [lax.ppermute(bufs[j], "seq", xor_pairs(seq, j)) for j in range(1, seq)]
        )
    prior = None
    for layer in range(layers):
        outs = layer_terms(
            layer, gathered[layer], key_weight, value_weight, prior, dec, enc, layer == layers - 1
        )
        prior = outs[0]
    received = [lax.ppermute(outs[j], "seq", xor_pairs(seq, j)) for j in range(1, seq)]
    enc_grad, gain = finish(outs[0], received, enc_final, norm_gain)
    for axis, size in (("dp", docs), ("seq", seq)):
        step = 1
        while step < size:
            gain = gain + lax.ppermute(gain, axis, xor_pairs(size, step))
            step *= 2
    return (enc_grad, gain[0] / docs)


def solution(mesh):
    placed = (
        P("dp", "seq", None),
        P(),
        P(None, "dp", "seq", None),
        P(None, "dp", "seq", None),
        P(None, "dp", "seq", None),
        P(None, "dp", "seq", None),
        P(None, None, "seq"),
        P(None, None, "seq"),
    )
    return jax.shard_map(
        body, mesh=mesh, in_specs=placed, out_specs=(P("dp", "seq", None), P()), check_vma=False
    )
```

```python
import functools

import jax
import jax.numpy as jnp
from jax import lax
from jax.experimental import pallas as pl
from jax.experimental.pallas import tpu as pltpu
from jax.sharding import PartitionSpec as P

HEAD_DIM = 64
LANES = 128
PROJ_BLOCK = 1024
ATTN_ROWS = 512
PACK_VMEM = 8 << 20
LAYER_VMEM = 32 << 20
F32 = jnp.float32
BF16 = jnp.bfloat16


def xor_pairs(size, step):
    return [(i, i ^ step) for i in range(size)]


def pack_layer(layer, arrays, seq_size):
    rows = [a.shape[2] for a in arrays]
    cols = arrays[0].shape[3] // seq_size
    total = sum(rows)

    def kernel(q_ref, g_ref, k_ref, v_ref, *rest):
        outs, sems = rest[:seq_size], rest[seq_size]
        me = lax.axis_index("seq")
        copies = []
        for j in list(range(1, seq_size)) + [0]:
            start = pl.multiple_of((me ^ j) * cols, LANES)
            base = 0
            for i, ref in enumerate((q_ref, g_ref, k_ref, v_ref)):
                copies.append(
                    pltpu.make_async_copy(
                        ref.at[layer, 0, :, pl.ds(start, cols)],
                        outs[j].at[pl.ds(base, rows[i]), :],
                        sems.at[j, i],
                    )
                )
                base += rows[i]
        for c in copies:
            c.start()
        for c in copies:
            c.wait()

    return pl.pallas_call(
        kernel,
        out_shape=[jax.ShapeDtypeStruct((total, cols), BF16)] * seq_size,
        in_specs=[pl.BlockSpec(memory_space=pltpu.HBM)] * 4,
        out_specs=[pl.BlockSpec(memory_space=pltpu.VMEM)] * seq_size,
        scratch_shapes=[pltpu.SemaphoreType.DMA((seq_size, 4))],
        compiler_params=pltpu.CompilerParams(vmem_limit_bytes=PACK_VMEM),
        name=f"pack_{layer}",
    )(*arrays)


def attention_into(bufs, dec, enc, kv_ref):
    cols = bufs[0].shape[1]
    count = len(bufs)
    per = LANES // HEAD_DIM
    group = max(1, ATTN_ROWS // dec)
    lane_head = lax.broadcasted_iota(jnp.int32, (1, LANES), 1) // HEAD_DIM
    rows = enc * count

    def stacked(base, ls):
        whole = jnp.concatenate([b[base : base + enc, ls].astype(F32) for b in bufs], axis=0)
        parts = [jnp.where(lane_head == h, whole, 0.0) for h in range(per)]
        return jnp.concatenate(parts, axis=0).astype(BF16)

    def chosen(stack):
        out = stack[:rows]
        for h in range(1, per):
            out = jnp.where(lane_head == h, stack[h * rows : (h + 1) * rows], out)
        return out.astype(BF16)

    nt = (((1,), (1,)), ((), ()))
    nn = (((1,), (0,)), ((), ()))
    for p in range(cols // LANES):
        ls = slice(p * LANES, (p + 1) * LANES)
        keys = stacked(2 * dec, ls)
        values = stacked(2 * dec + enc, ls)
        key_sum = value_sum = None
        for first in range(0, count, group):
            some = bufs[first : first + group]
            q = jnp.concatenate([b[0:dec, ls] for b in some], axis=0)
            g = jnp.concatenate([b[dec : 2 * dec, ls] for b in some], axis=0)
            width = q.shape[0]
            s = lax.dot_general(keys, q, nt, preferred_element_type=F32).reshape(per, rows, width)
            d = lax.dot_general(values, g, nt, preferred_element_type=F32).reshape(per, rows, width)
            e = jnp.exp(s - jnp.max(s, axis=1, keepdims=True))
            w = e * (1.0 / jnp.sum(e, axis=1, keepdims=True))
            delta = jnp.sum(w * d, axis=1, keepdims=True)
            ds = (w * (d - delta)).astype(BF16).reshape(per * rows, width)
            wl = w.astype(BF16).reshape(per * rows, width)
            vg = lax.dot_general(wl, g, nn, preferred_element_type=F32)
            kg = lax.dot_general(ds, q, nn, preferred_element_type=F32)
            key_sum = kg if key_sum is None else key_sum + kg
            value_sum = vg if value_sum is None else value_sum + vg
        kv_ref[:, ls] = chosen(key_sum)
        kv_ref[:, cols + p * LANES : cols + (p + 1) * LANES] = chosen(value_sum)


def layer_terms(layer, bufs, key_weight, value_weight, prior, dec, enc, last):
    count = len(bufs)
    width, cols = key_weight.shape[1], key_weight.shape[2]
    rows = enc * count
    block = PROJ_BLOCK
    nblocks = width // block

    def kernel(*refs):
        buf_refs = refs[:count]
        kw, vw = refs[count : count + 2]
        pos = count + 2
        if prior is not None:
            prior_ref = refs[pos]
            pos += 1
        n_out = count if last else 1
        outs = refs[pos : pos + n_out]
        pos += n_out
        w_ref, kv_ref, sems = refs[pos : pos + 3]
        copies = []
        for b in range(nblocks):
            pair = []
            for i, src in enumerate((kw, vw)):
                pair.append(
                    pltpu.make_async_copy(
                        src.at[layer, pl.ds(b * block, block), :],
                        w_ref.at[i, pl.ds(b * block, block), :],
                        sems.at[b, i],
                    )
                )
            copies.append(pair)
        for pair in copies:
            for c in pair:
                c.start()
        attention_into([r for r in buf_refs], dec, enc, kv_ref)
        nt = (((1,), (1,)), ((), ()))
        for b in range(nblocks):
            for c in copies[b]:
                c.wait()
            bs = slice(b * block, (b + 1) * block)
            acc = lax.dot_general(kv_ref[:, :cols], w_ref[0, bs, :], nt, preferred_element_type=F32)
            acc += lax.dot_general(kv_ref[:, cols:], w_ref[1, bs, :], nt, preferred_element_type=F32)
            if prior is not None:
                acc += prior_ref[:, bs]
            if last:
                for j in range(count):
                    piece = acc[j * enc : (j + 1) * enc]
                    outs[j][:, bs] = piece.astype(outs[j].dtype)
            else:
                outs[0][:, bs] = acc

    if last:
        out_shape = [jax.ShapeDtypeStruct((enc, width), F32 if j == 0 else BF16) for j in range(count)]
    else:
        out_shape = [jax.ShapeDtypeStruct((rows, width), F32)]
    vmem = pl.BlockSpec(memory_space=pltpu.VMEM)
    hbm = pl.BlockSpec(memory_space=pltpu.HBM)
    operands = list(bufs) + [key_weight, value_weight] + ([] if prior is None else [prior])
    return pl.pallas_call(
        kernel,
        out_shape=out_shape,
        in_specs=[vmem] * count + [hbm] * 2 + ([] if prior is None else [vmem]),
        out_specs=[vmem] * len(out_shape),
        scratch_shapes=[
            pltpu.VMEM((2, width, cols), BF16),
            pltpu.VMEM((rows, 2 * cols), BF16),
            pltpu.SemaphoreType.DMA((nblocks, 2)),
        ],
        compiler_params=pltpu.CompilerParams(vmem_limit_bytes=LAYER_VMEM),
        name=f"layer_{layer}",
    )(*operands)


def finish(own, received, enc_final, norm_gain):
    enc, width = own.shape

    def kernel(own_ref, *refs):
        recv_refs = refs[: len(received)]
        final_ref, gain_ref, grad_ref, term_ref = refs[len(received) :]
        state = own_ref[...]
        for r in recv_refs:
            state = state + r[...].astype(F32)
        final = final_ref[0].astype(F32)
        inv_rms = lax.rsqrt(jnp.mean(final * final, axis=-1, keepdims=True) + 1e-06)
        normed = final * inv_rms
        scaled = gain_ref[...] * state
        mean = jnp.mean(scaled * normed, axis=-1, keepdims=True)
        grad_ref[0] = (inv_rms * (scaled - normed * mean)).astype(BF16)
        term_ref[...] = jnp.sum(state * normed, axis=0, keepdims=True)

    return pl.pallas_call(
        kernel,
        out_shape=[
            jax.ShapeDtypeStruct((1, enc, width), BF16),
            jax.ShapeDtypeStruct((1, width), F32),
        ],
        compiler_params=pltpu.CompilerParams(vmem_limit_bytes=PACK_VMEM),
        name="finish",
    )(own, *received, enc_final, norm_gain.reshape(1, width))


def body(
    enc_final, norm_gain, dec_queries, out_grad, enc_keys, enc_values, key_weight, value_weight
):
    seq = lax.axis_size("seq")
    docs = lax.axis_size("dp")
    layers = dec_queries.shape[0]
    dec, enc = dec_queries.shape[2], enc_keys.shape[2]
    arrays = (dec_queries, out_grad, enc_keys, enc_values)
    gathered = []
    for layer in range(layers):
        bufs = pack_layer(layer, arrays, seq)
        gathered.append(
            [bufs[0]] + [lax.ppermute(bufs[j], "seq", xor_pairs(seq, j)) for j in range(1, seq)]
        )
    prior = None
    for layer in range(layers):
        outs = layer_terms(
            layer, gathered[layer], key_weight, value_weight, prior, dec, enc, layer == layers - 1
        )
        prior = outs[0]
    received = [lax.ppermute(outs[j], "seq", xor_pairs(seq, j)) for j in range(1, seq)]
    enc_grad, gain = finish(outs[0], received, enc_final, norm_gain)
    for axis, size in (("dp", docs), ("seq", seq)):
        step = 1
        while step < size:
            gain = gain + lax.ppermute(gain, axis, xor_pairs(size, step))
            step *= 2
    return (enc_grad, gain[0] / docs)


def solution(mesh):
    placed = (
        P("dp", "seq", None),
        P(),
        P(None, "dp", "seq", None),
        P(None, "dp", "seq", None),
        P(None, "dp", "seq", None),
        P(None, "dp", "seq", None),
        P(None, None, "seq"),
        P(None, None, "seq"),
    )
    return jax.shard_map(
        body, mesh=mesh, in_specs=placed, out_specs=(P("dp", "seq", None), P()), check_vma=False
    )
```

```python
import jax
import jax.numpy as jnp
from jax import lax
from jax.experimental import pallas as pl
from jax.experimental.pallas import tpu as pltpu
from jax.sharding import PartitionSpec as P

HEAD_DIM = 64
LANES = 128
PROJ_BLOCK = 1024
ATTN_ROWS = 512
PACK_VMEM = 8 << 20
LAYER_VMEM = 24 << 20
LOAD_VMEM = 8 << 20
F32 = jnp.float32
BF16 = jnp.bfloat16


def xor_pairs(size, step):
    return [(i, i ^ step) for i in range(size)]


def plan_chunks(layers, cols):
    chunks = [(layer, 0, cols) for layer in range(layers)]
    if cols > LANES:
        chunks[-1:] = [(layers - 1, 0, cols - LANES), (layers - 1, cols - LANES, LANES)]
    return chunks


def in_hbm(arrays):
    return [pltpu.with_memory_space_constraint(a, pltpu.HBM) for a in arrays]


def pack_chunk(index, chunk, arrays, seq_size):
    layer, first, width = chunk
    rows = [a.shape[2] for a in arrays]
    cols = arrays[0].shape[3] // seq_size

    def kernel(q_ref, g_ref, k_ref, v_ref, *rest):
        outs, sems = rest[:seq_size], rest[seq_size]
        me = lax.axis_index("seq")
        copies = []
        for j in list(range(1, seq_size)) + [0]:
            start = pl.multiple_of((me ^ j) * cols + first, LANES)
            base = 0
            for i, ref in enumerate((q_ref, g_ref, k_ref, v_ref)):
                copies.append(
                    pltpu.make_async_copy(
                        ref.at[layer, 0, :, pl.ds(start, width)],
                        outs[j].at[pl.ds(base, rows[i]), :],
                        sems.at[j, i],
                    )
                )
                base += rows[i]
        for c in copies:
            c.start()
        for c in copies:
            c.wait()

    return pl.pallas_call(
        kernel,
        out_shape=[jax.ShapeDtypeStruct((sum(rows), width), BF16)] * seq_size,
        in_specs=[pl.BlockSpec(memory_space=pltpu.HBM)] * 4,
        out_specs=[pl.BlockSpec(memory_space=pltpu.VMEM)] * seq_size,
        scratch_shapes=[pltpu.SemaphoreType.DMA((seq_size, 4))],
        compiler_params=pltpu.CompilerParams(vmem_limit_bytes=PACK_VMEM),
        name=f"pack_{index}",
    )(*in_hbm(arrays))


def load_weights(chunks, key_weight, value_weight, after):
    width = key_weight.shape[1]

    def kernel(kw, vw, after_ref, *rest):
        outs, sems = rest[: len(chunks)], rest[len(chunks)]
        copies = []
        for n, (layer, first, cols) in enumerate(chunks):
            for i, src in enumerate((kw, vw)):
                copies.append(
                    pltpu.make_async_copy(
                        src.at[layer, :, pl.ds(first, cols)],
                        outs[n].at[:, pl.ds(i * cols, cols)],
                        sems.at[n, i],
                    )
                )
        for c in copies:
            c.start()
        for c in copies:
            c.wait()

    total = 4 * key_weight.size
    return pl.pallas_call(
        kernel,
        out_shape=[jax.ShapeDtypeStruct((width, 2 * cols), BF16) for _, _, cols in chunks],
        in_specs=[pl.BlockSpec(memory_space=pltpu.HBM)] * 2 + [pl.BlockSpec(memory_space=pl.ANY)],
        out_specs=[pl.BlockSpec(memory_space=pltpu.VMEM)] * len(chunks),
        scratch_shapes=[pltpu.SemaphoreType.DMA((len(chunks), 2))],
        compiler_params=pltpu.CompilerParams(vmem_limit_bytes=LOAD_VMEM),
        cost_estimate=pl.CostEstimate(flops=0, transcendentals=0, bytes_accessed=total),
        name="load_weights",
    )(*in_hbm([key_weight, value_weight]), after)


def attention_into(bufs, dec, enc, kv_ref):
    cols = bufs[0].shape[1]
    count = len(bufs)
    per = LANES // HEAD_DIM
    group = max(1, ATTN_ROWS // dec)
    lane_head = lax.broadcasted_iota(jnp.int32, (1, LANES), 1) // HEAD_DIM
    rows = enc * count

    def stacked(base, ls):
        whole = jnp.concatenate([b[base : base + enc, ls].astype(F32) for b in bufs], axis=0)
        parts = [jnp.where(lane_head == h, whole, 0.0) for h in range(per)]
        return jnp.concatenate(parts, axis=0).astype(BF16)

    def chosen(stack):
        out = stack[:rows]
        for h in range(1, per):
            out = jnp.where(lane_head == h, stack[h * rows : (h + 1) * rows], out)
        return out.astype(BF16)

    nt = (((1,), (1,)), ((), ()))
    nn = (((1,), (0,)), ((), ()))
    for p in range(cols // LANES):
        ls = slice(p * LANES, (p + 1) * LANES)
        keys = stacked(2 * dec, ls)
        values = stacked(2 * dec + enc, ls)
        key_sum = value_sum = None
        for first in range(0, count, group):
            some = bufs[first : first + group]
            q = jnp.concatenate([b[0:dec, ls] for b in some], axis=0)
            g = jnp.concatenate([b[dec : 2 * dec, ls] for b in some], axis=0)
            width = q.shape[0]
            s = lax.dot_general(keys, q, nt, preferred_element_type=F32).reshape(per, rows, width)
            d = lax.dot_general(values, g, nt, preferred_element_type=F32).reshape(per, rows, width)
            e = jnp.exp(s - jnp.max(s, axis=1, keepdims=True))
            w = e * (1.0 / jnp.sum(e, axis=1, keepdims=True))
            delta = jnp.sum(w * d, axis=1, keepdims=True)
            ds = (w * (d - delta)).astype(BF16).reshape(per * rows, width)
            wl = w.astype(BF16).reshape(per * rows, width)
            vg = lax.dot_general(wl, g, nn, preferred_element_type=F32)
            kg = lax.dot_general(ds, q, nn, preferred_element_type=F32)
            key_sum = kg if key_sum is None else key_sum + kg
            value_sum = vg if value_sum is None else value_sum + vg
        kv_ref[:, ls] = chosen(key_sum)
        kv_ref[:, cols + p * LANES : cols + (p + 1) * LANES] = chosen(value_sum)


def chunk_terms(index, bufs, weight, prior, dec, enc, last):
    count = len(bufs)
    width = weight.shape[0]
    rows = enc * count
    block = PROJ_BLOCK

    def kernel(*refs):
        buf_refs, w_ref = refs[:count], refs[count]
        pos = count + 1
        if prior is not None:
            prior_ref = refs[pos]
            pos += 1
        outs, kv_ref = refs[pos:-1], refs[-1]
        attention_into(buf_refs, dec, enc, kv_ref)
        nt = (((1,), (1,)), ((), ()))
        for b in range(width // block):
            bs = slice(b * block, (b + 1) * block)
            acc = lax.dot_general(kv_ref[...], w_ref[bs, :], nt, preferred_element_type=F32)
            if prior is not None:
                acc += prior_ref[:, bs]
            if last:
                for j in range(count):
                    outs[j][:, bs] = acc[j * enc : (j + 1) * enc].astype(outs[j].dtype)
            else:
                outs[0][:, bs] = acc

    if last:
        out_shape = [jax.ShapeDtypeStruct((enc, width), F32 if j == 0 else BF16) for j in range(count)]
    else:
        out_shape = [jax.ShapeDtypeStruct((rows, width), F32)]
    vmem = pl.BlockSpec(memory_space=pltpu.VMEM)
    operands = list(bufs) + [weight] + ([] if prior is None else [prior])
    return pl.pallas_call(
        kernel,
        out_shape=out_shape,
        in_specs=[vmem] * len(operands),
        out_specs=[vmem] * len(out_shape),
        scratch_shapes=[pltpu.VMEM((rows, weight.shape[1]), BF16)],
        compiler_params=pltpu.CompilerParams(vmem_limit_bytes=LAYER_VMEM),
        name=f"chunk_{index}",
    )(*operands)


def finish(own, received, enc_final, norm_gain):
    enc, width = own.shape

    def kernel(own_ref, *refs):
        recv_refs = refs[: len(received)]
        final_ref, gain_ref, grad_ref, term_ref = refs[len(received) :]
        state = own_ref[...]
        for r in recv_refs:
            state = state + r[...].astype(F32)
        final = final_ref[0].astype(F32)
        inv_rms = lax.rsqrt(jnp.mean(final * final, axis=-1, keepdims=True) + 1e-06)
        normed = final * inv_rms
        scaled = gain_ref[...] * state
        mean = jnp.mean(scaled * normed, axis=-1, keepdims=True)
        grad_ref[0] = (inv_rms * (scaled - normed * mean)).astype(BF16)
        term_ref[...] = jnp.sum(state * normed, axis=0, keepdims=True)

    return pl.pallas_call(
        kernel,
        out_shape=[
            jax.ShapeDtypeStruct((1, enc, width), BF16),
            jax.ShapeDtypeStruct((1, width), F32),
        ],
        compiler_params=pltpu.CompilerParams(vmem_limit_bytes=PACK_VMEM),
        name="finish",
    )(own, *received, enc_final, norm_gain.reshape(1, width))


def body(
    enc_final, norm_gain, dec_queries, out_grad, enc_keys, enc_values, key_weight, value_weight
):
    seq = lax.axis_size("seq")
    docs = lax.axis_size("dp")
    layers = dec_queries.shape[0]
    dec, enc = dec_queries.shape[2], enc_keys.shape[2]
    arrays = (dec_queries, out_grad, enc_keys, enc_values)
    chunks = plan_chunks(layers, key_weight.shape[2])
    gathered = []
    for index, chunk in enumerate(chunks):
        bufs = pack_chunk(index, chunk, arrays, seq)
        gathered.append(
            [bufs[0]] + [lax.ppermute(bufs[j], "seq", xor_pairs(seq, j)) for j in range(1, seq)]
        )
    weights = load_weights(chunks, key_weight, value_weight, gathered[-1][0])
    prior = None
    for index in range(len(chunks)):
        outs = chunk_terms(
            index, gathered[index], weights[index], prior, dec, enc, index == len(chunks) - 1
        )
        prior = outs[0]
    received = [lax.ppermute(outs[j], "seq", xor_pairs(seq, j)) for j in range(1, seq)]
    enc_grad, gain = finish(outs[0], received, enc_final, norm_gain)
    for axis, size in (("dp", docs), ("seq", seq)):
        step = 1
        while step < size:
            gain = gain + lax.ppermute(gain, axis, xor_pairs(size, step))
            step *= 2
    return (enc_grad, gain[0] / docs)


def solution(mesh):
    placed = (
        P("dp", "seq", None),
        P(),
        P(None, "dp", "seq", None),
        P(None, "dp", "seq", None),
        P(None, "dp", "seq", None),
        P(None, "dp", "seq", None),
        P(None, None, "seq"),
        P(None, None, "seq"),
    )
    return jax.shard_map(
        body, mesh=mesh, in_specs=placed, out_specs=(P("dp", "seq", None), P()), check_vma=False
    )
```

```python
import jax
import jax.numpy as jnp
from jax import lax
from jax.experimental import pallas as pl
from jax.experimental.pallas import tpu as pltpu
from jax.sharding import PartitionSpec as P


HEAD_DIM = 64
LANES = 128
PROJ_BLOCK = 1024
ATTN_ROWS = 512
PACK_VMEM = 8 << 20
LAYER_VMEM = 24 << 20
LOAD_VMEM = 8 << 20
SMALL_VMEM = 2 << 20
F32 = jnp.float32
BF16 = jnp.bfloat16


def xor_pairs(size, step):
    return [(i, i ^ step) for i in range(size)]


def exchange(value, axis, size, step):
    return lax.ppermute(value, axis, xor_pairs(size, step))


def plan_chunks(layers, cols):
    chunks = [(layer, 0, cols) for layer in range(layers)]
    if cols > LANES:
        chunks[-1:] = [(layers - 1, 0, cols - LANES), (layers - 1, cols - LANES, LANES)]
    return chunks


def in_hbm(arrays):
    return [pltpu.with_memory_space_constraint(a, pltpu.HBM) for a in arrays]


def pack_chunk(chunk, arrays, seq_size):
    layer, first, width = chunk
    rows = [a.shape[2] for a in arrays]
    cols = arrays[0].shape[3] // seq_size

    def kernel(q_ref, g_ref, k_ref, v_ref, *rest):
        outs, sems = rest[:seq_size], rest[seq_size]
        me = lax.axis_index("seq")
        copies = []
        for j in list(range(1, seq_size)) + [0]:
            start = pl.multiple_of((me ^ j) * cols + first, LANES)
            base = 0
            for i, ref in enumerate((q_ref, g_ref, k_ref, v_ref)):
                copies.append(
                    pltpu.make_async_copy(
                        ref.at[layer, 0, :, pl.ds(start, width)],
                        outs[j].at[pl.ds(base, rows[i]), :],
                        sems.at[j, i],
                    )
                )
                base += rows[i]
        for c in copies:
            c.start()
        for c in copies:
            c.wait()

    return pl.pallas_call(
        kernel,
        out_shape=[jax.ShapeDtypeStruct((sum(rows), width), BF16)] * seq_size,
        in_specs=[pl.BlockSpec(memory_space=pltpu.HBM)] * 4,
        out_specs=[pl.BlockSpec(memory_space=pltpu.VMEM)] * seq_size,
        scratch_shapes=[pltpu.SemaphoreType.DMA((seq_size, 4))],
        compiler_params=pltpu.CompilerParams(vmem_limit_bytes=PACK_VMEM),
    )(*in_hbm(arrays))


def load_weights(chunks, key_weight, value_weight, after):
    width = key_weight.shape[1]

    def kernel(kw, vw, after_ref, *rest):
        outs, sems = rest[: len(chunks)], rest[len(chunks)]
        copies = []
        for n, (layer, first, cols) in enumerate(chunks):
            for i, src in enumerate((kw, vw)):
                copies.append(
                    pltpu.make_async_copy(
                        src.at[layer, :, pl.ds(first, cols)],
                        outs[n].at[:, pl.ds(i * cols, cols)],
                        sems.at[n, i],
                    )
                )
        for c in copies:
            c.start()
        for c in copies:
            c.wait()

    total = 4 * key_weight.size
    return pl.pallas_call(
        kernel,
        out_shape=[jax.ShapeDtypeStruct((width, 2 * cols), BF16) for _, _, cols in chunks],
        in_specs=[pl.BlockSpec(memory_space=pltpu.HBM)] * 2 + [pl.BlockSpec(memory_space=pl.ANY)],
        out_specs=[pl.BlockSpec(memory_space=pltpu.VMEM)] * len(chunks),
        scratch_shapes=[pltpu.SemaphoreType.DMA((len(chunks), 2))],
        compiler_params=pltpu.CompilerParams(vmem_limit_bytes=LOAD_VMEM),
        cost_estimate=pl.CostEstimate(flops=0, transcendentals=0, bytes_accessed=total),
        name="load_weights",
    )(*in_hbm([key_weight, value_weight]), after)


def attention_into(bufs, dec, enc, kv_ref):
    cols = bufs[0].shape[1]
    count = len(bufs)
    per = LANES // HEAD_DIM
    group = max(1, ATTN_ROWS // dec)
    lane_head = lax.broadcasted_iota(jnp.int32, (1, LANES), 1) // HEAD_DIM
    rows = enc * count

    def stacked(base, ls):
        whole = jnp.concatenate([b[base : base + enc, ls].astype(F32) for b in bufs], axis=0)
        parts = [jnp.where(lane_head == h, whole, 0.0) for h in range(per)]
        return jnp.concatenate(parts, axis=0).astype(BF16)

    def chosen(stack):
        out = stack[:rows]
        for h in range(1, per):
            out = jnp.where(lane_head == h, stack[h * rows : (h + 1) * rows], out)
        return out.astype(BF16)

    nt = (((1,), (1,)), ((), ()))
    nn = (((1,), (0,)), ((), ()))
    for p in range(cols // LANES):
        ls = slice(p * LANES, (p + 1) * LANES)
        keys = stacked(2 * dec, ls)
        values = stacked(2 * dec + enc, ls)
        key_sum = value_sum = None
        for first in range(0, count, group):
            some = bufs[first : first + group]
            q = jnp.concatenate([b[0:dec, ls] for b in some], axis=0)
            g = jnp.concatenate([b[dec : 2 * dec, ls] for b in some], axis=0)
            width = q.shape[0]
            s = lax.dot_general(keys, q, nt, preferred_element_type=F32).reshape(per, rows, width)
            d = lax.dot_general(values, g, nt, preferred_element_type=F32).reshape(per, rows, width)
            e = jnp.exp(s - jnp.max(s, axis=1, keepdims=True))
            w = e * (1.0 / jnp.sum(e, axis=1, keepdims=True))
            delta = jnp.sum(w * d, axis=1, keepdims=True)
            ds = (w * (d - delta)).astype(BF16).reshape(per * rows, width)
            wl = w.astype(BF16).reshape(per * rows, width)
            vg = lax.dot_general(wl, g, nn, preferred_element_type=F32)
            kg = lax.dot_general(ds, q, nn, preferred_element_type=F32)
            key_sum = kg if key_sum is None else key_sum + kg
            value_sum = vg if value_sum is None else value_sum + vg
        kv_ref[:, ls] = chosen(key_sum)
        kv_ref[:, cols + p * LANES : cols + (p + 1) * LANES] = chosen(value_sum)


def chunk_terms(bufs, weight, prior, dec, enc, last):
    count = len(bufs)
    width = weight.shape[0]
    rows = enc * count
    block = PROJ_BLOCK

    def kernel(*refs):
        buf_refs, w_ref = refs[:count], refs[count]
        pos = count + 1
        if prior is not None:
            prior_ref = refs[pos]
            pos += 1
        outs, kv_ref = refs[pos:-1], refs[-1]
        attention_into(buf_refs, dec, enc, kv_ref)
        nt = (((1,), (1,)), ((), ()))
        for b in range(width // block):
            bs = slice(b * block, (b + 1) * block)
            acc = lax.dot_general(kv_ref[...], w_ref[bs, :], nt, preferred_element_type=F32)
            if prior is not None:
                acc += prior_ref[:, bs]
            if last:
                for j in range(count):
                    outs[j][:, bs] = acc[j * enc : (j + 1) * enc].astype(outs[j].dtype)
            else:
                outs[0][:, bs] = acc

    if last:
        out_shape = [jax.ShapeDtypeStruct((enc, width), F32 if j == 0 else BF16) for j in range(count)]
    else:
        out_shape = [jax.ShapeDtypeStruct((rows, width), F32)]
    vmem = pl.BlockSpec(memory_space=pltpu.VMEM)
    operands = list(bufs) + [weight] + ([] if prior is None else [prior])
    return pl.pallas_call(
        kernel,
        out_shape=out_shape,
        in_specs=[vmem] * len(operands),
        out_specs=[vmem] * len(out_shape),
        scratch_shapes=[pltpu.VMEM((rows, weight.shape[1]), BF16)],
        compiler_params=pltpu.CompilerParams(vmem_limit_bytes=LAYER_VMEM),
    )(*operands)


def split_final(enc_final, after):
    enc, half = enc_final.shape[1], enc_final.shape[2] // 2

    def kernel(src, after_ref, *rest):
        outs, sems = rest[:2], rest[2]
        copies = [
            pltpu.make_async_copy(src.at[0, :, pl.ds(h * half, half)], outs[h], sems.at[h])
            for h in range(2)
        ]
        for c in copies:
            c.start()
        for c in copies:
            c.wait()

    return pl.pallas_call(
        kernel,
        out_shape=[jax.ShapeDtypeStruct((enc, half), BF16)] * 2,
        in_specs=[pl.BlockSpec(memory_space=pltpu.HBM), pl.BlockSpec(memory_space=pl.ANY)],
        out_specs=[pl.BlockSpec(memory_space=pltpu.VMEM)] * 2,
        scratch_shapes=[pltpu.SemaphoreType.DMA((2,))],
        compiler_params=pltpu.CompilerParams(vmem_limit_bytes=SMALL_VMEM),
        name="split_final",
    )(*in_hbm([enc_final]), after)


def gather_rows(mine, seq_size, steps):
    have = [(0, mine)]
    for n, step in enumerate(steps):
        whole = have[0][1] if n == 0 else jnp.concatenate([a for _, a in have], axis=0)
        have = have + [(step, exchange(whole, "seq", seq_size, step))]
    return have


def row_order(steps):
    order = [0]
    for step in steps:
        order = order + [j ^ step for j in order]
    return order


def gain_terms(pieces, halves, orders):
    count = len(pieces)
    enc, width = pieces[0].shape
    half = width // 2
    sizes = [len(parts) for parts in halves]

    def kernel(*refs):
        piece_refs = refs[:count]
        part_refs = [refs[count : count + sizes[0]], refs[count + sizes[0] : count + sum(sizes)]]
        out_ref = refs[-1]
        blocks = [[None] * count, [None] * count]
        for h in range(2):
            place = 0
            for ref in part_refs[h]:
                for k in range(ref.shape[0] // enc):
                    blocks[h][orders[h][place]] = (ref, k * enc)
                    place += 1
        inv = []
        for j in range(count):
            square = None
            for h in range(2):
                ref, base = blocks[h][j]
                x = ref[pl.ds(base, enc), :].astype(F32)
                total = jnp.sum(x * x, axis=-1, keepdims=True)
                square = total if square is None else square + total
            inv.append(lax.rsqrt(square * (1.0 / width) + 1e-06))
        for h in range(2):
            hs = slice(h * half, (h + 1) * half)
            terms = None
            for j in range(count):
                ref, base = blocks[h][j]
                normed = ref[pl.ds(base, enc), :].astype(F32) * inv[j]
                product = piece_refs[j][:, hs].astype(F32) * normed
                terms = product if terms is None else terms + product
            out_ref[:, hs] = jnp.sum(terms, axis=0, keepdims=True)

    return pl.pallas_call(
        kernel,
        out_shape=jax.ShapeDtypeStruct((1, width), F32),
        compiler_params=pltpu.CompilerParams(vmem_limit_bytes=PACK_VMEM),
        name="gain_terms",
    )(*pieces, *[a for parts in halves for a in parts])


def finish(own, received, enc_final, norm_gain):
    enc, width = own.shape

    def kernel(own_ref, *refs):
        recv_refs = refs[: len(received)]
        final_ref, gain_ref, grad_ref = refs[len(received) :]
        state = own_ref[...]
        for r in recv_refs:
            state = state + r[...].astype(F32)
        final = final_ref[0].astype(F32)
        inv_rms = lax.rsqrt(jnp.mean(final * final, axis=-1, keepdims=True) + 1e-06)
        normed = final * inv_rms
        scaled = gain_ref[...] * state
        mean = jnp.mean(scaled * normed, axis=-1, keepdims=True)
        grad_ref[0] = (inv_rms * (scaled - normed * mean)).astype(BF16)

    return pl.pallas_call(
        kernel,
        out_shape=jax.ShapeDtypeStruct((1, enc, width), BF16),
        compiler_params=pltpu.CompilerParams(vmem_limit_bytes=PACK_VMEM),
        name="finish",
    )(own, *received, enc_final, norm_gain.reshape(1, width))


def body(
    enc_final, norm_gain, dec_queries, out_grad, enc_keys, enc_values, key_weight, value_weight
):
    seq = lax.axis_size("seq")
    docs = lax.axis_size("dp")
    layers = dec_queries.shape[0]
    dec, enc = dec_queries.shape[2], enc_keys.shape[2]
    arrays = (dec_queries, out_grad, enc_keys, enc_values)
    chunks = plan_chunks(layers, key_weight.shape[2])
    gathered = []
    for index, chunk in enumerate(chunks):
        bufs = pack_chunk(chunk, arrays, seq)
        gathered.append([bufs[0]] + [exchange(bufs[j], "seq", seq, j) for j in range(1, seq)])
        if index == 0:
            steps = [1 << b for b in range(seq.bit_length() - 1)]
            orders = [steps, steps[::-1]]
            finals = split_final(enc_final, bufs[0])
            halves = [gather_rows(f, seq, o) for f, o in zip(finals, orders)]
    weights = load_weights(chunks, key_weight, value_weight, gathered[-1][0])
    prior = None
    for index in range(len(chunks)):
        outs = chunk_terms(
            gathered[index], weights[index], prior, dec, enc, index == len(chunks) - 1
        )
        prior = outs[0]
    received = [exchange(outs[j], "seq", seq, j) for j in range(1, seq)]
    gain = gain_terms(
        outs, [[a for _, a in parts] for parts in halves], [row_order(o) for o in orders]
    )
    enc_grad = finish(outs[0], received, enc_final, norm_gain)
    stages = [
        (axis, size, 1 << b)
        for axis, size in (("dp", docs), ("seq", seq))
        for b in range(size.bit_length() - 1)
    ]
    for axis, size, step in stages:
        gain = gain + exchange(gain, axis, size, step)
    return (enc_grad, gain[0] / docs)


def solution(mesh):
    placed = (
        P("dp", "seq", None),
        P(),
        P(None, "dp", "seq", None),
        P(None, "dp", "seq", None),
        P(None, "dp", "seq", None),
        P(None, "dp", "seq", None),
        P(None, None, "seq"),
        P(None, None, "seq"),
    )

    def whole(*args):
        step = jax.shard_map(
            body, mesh=mesh, in_specs=placed, out_specs=(P("dp", "seq", None), P()), check_vma=False
        )
        return step(*args)

    return whole
```

```python
import jax
import jax.numpy as jnp
from jax import lax
from jax.experimental import pallas as pl
from jax.experimental.pallas import tpu as pltpu
from jax.sharding import PartitionSpec as P


HEAD_DIM = 64
LANES = 128
PROJ_BLOCK = 1024
ATTN_ROWS = 512
PACK_VMEM = 8 << 20
LAYER_VMEM = 24 << 20
SMALL_VMEM = 2 << 20
F32 = jnp.float32
BF16 = jnp.bfloat16


def xor_pairs(size, step):
    return [(i, i ^ step) for i in range(size)]


def exchange(value, axis, size, step):
    return lax.ppermute(value, axis, xor_pairs(size, step))


def plan_chunks(layers, cols):
    chunks = [(layer, 0, cols) for layer in range(layers)]
    if cols > LANES:
        chunks[-1:] = [(layers - 1, 0, cols - LANES), (layers - 1, cols - LANES, LANES)]
    return chunks


def in_hbm(arrays):
    return [pltpu.with_memory_space_constraint(a, pltpu.HBM) for a in arrays]


def pack_chunk(chunk, arrays, seq_size):
    layer, first, width = chunk
    rows = [a.shape[2] for a in arrays]
    cols = arrays[0].shape[3] // seq_size

    def kernel(q_ref, g_ref, k_ref, v_ref, *rest):
        outs, sems = rest[:seq_size], rest[seq_size]
        me = lax.axis_index("seq")
        copies = []
        for j in list(range(1, seq_size)) + [0]:
            start = pl.multiple_of((me ^ j) * cols + first, LANES)
            base = 0
            for i, ref in enumerate((q_ref, g_ref, k_ref, v_ref)):
                copies.append(
                    pltpu.make_async_copy(
                        ref.at[layer, 0, :, pl.ds(start, width)],
                        outs[j].at[pl.ds(base, rows[i]), :],
                        sems.at[j, i],
                    )
                )
                base += rows[i]
        for c in copies:
            c.start()
        for c in copies:
            c.wait()

    return pl.pallas_call(
        kernel,
        out_shape=[jax.ShapeDtypeStruct((sum(rows), width), BF16)] * seq_size,
        in_specs=[pl.BlockSpec(memory_space=pltpu.HBM)] * 4,
        out_specs=[pl.BlockSpec(memory_space=pltpu.VMEM)] * seq_size,
        scratch_shapes=[pltpu.SemaphoreType.DMA((seq_size, 4))],
        compiler_params=pltpu.CompilerParams(vmem_limit_bytes=PACK_VMEM),
    )(*in_hbm(arrays))


def attention_into(bufs, dec, enc, kv_ref):
    cols = bufs[0].shape[1]
    count = len(bufs)
    per = LANES // HEAD_DIM
    group = max(1, ATTN_ROWS // dec)
    lane_head = lax.broadcasted_iota(jnp.int32, (1, LANES), 1) // HEAD_DIM
    rows = enc * count

    def stacked(base, ls):
        whole = jnp.concatenate([b[base : base + enc, ls].astype(F32) for b in bufs], axis=0)
        parts = [jnp.where(lane_head == h, whole, 0.0) for h in range(per)]
        return jnp.concatenate(parts, axis=0).astype(BF16)

    def chosen(stack):
        out = stack[:rows]
        for h in range(1, per):
            out = jnp.where(lane_head == h, stack[h * rows : (h + 1) * rows], out)
        return out.astype(BF16)

    nt = (((1,), (1,)), ((), ()))
    nn = (((1,), (0,)), ((), ()))
    for p in range(cols // LANES):
        ls = slice(p * LANES, (p + 1) * LANES)
        keys = stacked(2 * dec, ls)
        values = stacked(2 * dec + enc, ls)
        key_sum = value_sum = None
        for first in range(0, count, group):
            some = bufs[first : first + group]
            q = jnp.concatenate([b[0:dec, ls] for b in some], axis=0)
            g = jnp.concatenate([b[dec : 2 * dec, ls] for b in some], axis=0)
            width = q.shape[0]
            s = lax.dot_general(keys, q, nt, preferred_element_type=F32).reshape(per, rows, width)
            d = lax.dot_general(values, g, nt, preferred_element_type=F32).reshape(per, rows, width)
            e = jnp.exp(s - jnp.max(s, axis=1, keepdims=True))
            w = e * (1.0 / jnp.sum(e, axis=1, keepdims=True))
            delta = jnp.sum(w * d, axis=1, keepdims=True)
            ds = (w * (d - delta)).astype(BF16).reshape(per * rows, width)
            wl = w.astype(BF16).reshape(per * rows, width)
            vg = lax.dot_general(wl, g, nn, preferred_element_type=F32)
            kg = lax.dot_general(ds, q, nn, preferred_element_type=F32)
            key_sum = kg if key_sum is None else key_sum + kg
            value_sum = vg if value_sum is None else value_sum + vg
        kv_ref[:, ls] = chosen(key_sum)
        kv_ref[:, cols + p * LANES : cols + (p + 1) * LANES] = chosen(value_sum)


def weight_copies(chunk, key_weight, value_weight, dest, sems):
    layer, first, cols = chunk
    copies = []
    for b in range(dest.shape[0] // PROJ_BLOCK):
        rows = pl.ds(b * PROJ_BLOCK, PROJ_BLOCK)
        copies.append(
            [
                pltpu.make_async_copy(
                    src.at[layer, rows, pl.ds(first, cols)],
                    dest.at[rows, pl.ds(i * cols, cols)],
                    sems.at[b, i],
                )
                for i, src in enumerate((key_weight, value_weight))
            ]
        )
    return copies


def chunk_terms(index, chunks, bufs, key_weight, value_weight, ready, prior, dec, enc):
    count = len(bufs)
    width = key_weight.shape[1]
    rows = enc * count
    nblocks = width // PROJ_BLOCK
    cols = chunks[index][2]
    last = index == len(chunks) - 1
    fetch = index == 0 and not last

    def kernel(*refs):
        refs = list(refs)
        buf_refs = [refs.pop(0) for _ in range(count)]
        if ready is None:
            kw, vw = refs.pop(0), refs.pop(0)
        else:
            w_ref = refs.pop(0)
        prior_ref = None if prior is None else refs.pop(0)
        outs = [refs.pop(0) for _ in range(count if last else 1)]
        next_ref = refs.pop(0) if fetch else None
        kv_ref = refs.pop(0)
        if ready is None:
            w_ref, sems = refs.pop(0), refs.pop(0)
            copies = weight_copies(chunks[index], kw, vw, w_ref, sems)
            for pair in copies:
                for c in pair:
                    c.start()
        if fetch:
            next_copies = weight_copies(chunks[-1], kw, vw, next_ref, refs.pop(0))
            for pair in next_copies:
                for c in pair:
                    c.start()
        attention_into(buf_refs, dec, enc, kv_ref)
        nt = (((1,), (1,)), ((), ()))
        for b in range(nblocks):
            bs = slice(b * PROJ_BLOCK, (b + 1) * PROJ_BLOCK)
            if ready is None:
                for c in copies[b]:
                    c.wait()
            acc = lax.dot_general(kv_ref[...], w_ref[bs, :], nt, preferred_element_type=F32)
            if prior is not None:
                acc += prior_ref[:, bs]
            if last:
                for j in range(count):
                    outs[j][:, bs] = acc[j * enc : (j + 1) * enc].astype(outs[j].dtype)
            else:
                outs[0][:, bs] = acc
        if fetch:
            for pair in next_copies:
                for c in pair:
                    c.wait()

    if last:
        out_shape = [jax.ShapeDtypeStruct((enc, width), F32 if j == 0 else BF16) for j in range(count)]
    else:
        out_shape = [jax.ShapeDtypeStruct((rows, width), F32)]
    scratch = [pltpu.VMEM((rows, 2 * cols), BF16)]
    if ready is None:
        scratch += [pltpu.VMEM((width, 2 * cols), BF16), pltpu.SemaphoreType.DMA((nblocks, 2))]
    if fetch:
        out_shape.append(jax.ShapeDtypeStruct((width, 2 * chunks[-1][2]), BF16))
        scratch.append(pltpu.SemaphoreType.DMA((nblocks, 2)))
    vmem = pl.BlockSpec(memory_space=pltpu.VMEM)
    if ready is None:
        weights, specs = in_hbm([key_weight, value_weight]), [pl.BlockSpec(memory_space=pltpu.HBM)] * 2
    else:
        weights, specs = [ready], [vmem]
    tail = [] if prior is None else [prior]
    return pl.pallas_call(
        kernel,
        out_shape=out_shape,
        in_specs=[vmem] * count + specs + [vmem] * len(tail),
        out_specs=[vmem] * len(out_shape),
        scratch_shapes=scratch,
        compiler_params=pltpu.CompilerParams(vmem_limit_bytes=LAYER_VMEM),
    )(*bufs, *weights, *tail)


def split_final(enc_final, after):
    enc, half = enc_final.shape[1], enc_final.shape[2] // 2

    def kernel(src, after_ref, *rest):
        outs, sems = rest[:2], rest[2]
        copies = [
            pltpu.make_async_copy(src.at[0, :, pl.ds(h * half, half)], outs[h], sems.at[h])
            for h in range(2)
        ]
        for c in copies:
            c.start()
        for c in copies:
            c.wait()

    return pl.pallas_call(
        kernel,
        out_shape=[jax.ShapeDtypeStruct((enc, half), BF16)] * 2,
        in_specs=[pl.BlockSpec(memory_space=pltpu.HBM), pl.BlockSpec(memory_space=pl.ANY)],
        out_specs=[pl.BlockSpec(memory_space=pltpu.VMEM)] * 2,
        scratch_shapes=[pltpu.SemaphoreType.DMA((2,))],
        compiler_params=pltpu.CompilerParams(vmem_limit_bytes=SMALL_VMEM),
        name="split_final",
    )(*in_hbm([enc_final]), after)


def gather_rows(mine, seq_size, steps):
    have = [(0, mine)]
    for n, step in enumerate(steps):
        whole = have[0][1] if n == 0 else jnp.concatenate([a for _, a in have], axis=0)
        have = have + [(step, exchange(whole, "seq", seq_size, step))]
    return have


def row_order(steps):
    order = [0]
    for step in steps:
        order = order + [j ^ step for j in order]
    return order


def gain_terms(pieces, halves, orders):
    count = len(pieces)
    enc, width = pieces[0].shape
    half = width // 2
    sizes = [len(parts) for parts in halves]

    def kernel(*refs):
        piece_refs = refs[:count]
        part_refs = [refs[count : count + sizes[0]], refs[count + sizes[0] : count + sum(sizes)]]
        out_ref = refs[-1]
        blocks = [[None] * count, [None] * count]
        for h in range(2):
            place = 0
            for ref in part_refs[h]:
                for k in range(ref.shape[0] // enc):
                    blocks[h][orders[h][place]] = (ref, k * enc)
                    place += 1
        inv = []
        for j in range(count):
            square = None
            for h in range(2):
                ref, base = blocks[h][j]
                x = ref[pl.ds(base, enc), :].astype(F32)
                total = jnp.sum(x * x, axis=-1, keepdims=True)
                square = total if square is None else square + total
            inv.append(lax.rsqrt(square * (1.0 / width) + 1e-06))
        for h in range(2):
            hs = slice(h * half, (h + 1) * half)
            terms = None
            for j in range(count):
                ref, base = blocks[h][j]
                normed = ref[pl.ds(base, enc), :].astype(F32) * inv[j]
                product = piece_refs[j][:, hs].astype(F32) * normed
                terms = product if terms is None else terms + product
            out_ref[:, hs] = jnp.sum(terms, axis=0, keepdims=True)

    return pl.pallas_call(
        kernel,
        out_shape=jax.ShapeDtypeStruct((1, width), F32),
        compiler_params=pltpu.CompilerParams(vmem_limit_bytes=PACK_VMEM),
        name="gain_terms",
    )(*pieces, *[a for parts in halves for a in parts])


def finish(own, received, enc_final, norm_gain):
    enc, width = own.shape

    def kernel(own_ref, *refs):
        recv_refs = refs[: len(received)]
        final_ref, gain_ref, grad_ref = refs[len(received) :]
        state = own_ref[...]
        for r in recv_refs:
            state = state + r[...].astype(F32)
        final = final_ref[0].astype(F32)
        inv_rms = lax.rsqrt(jnp.mean(final * final, axis=-1, keepdims=True) + 1e-06)
        normed = final * inv_rms
        scaled = gain_ref[...] * state
        mean = jnp.mean(scaled * normed, axis=-1, keepdims=True)
        grad_ref[0] = (inv_rms * (scaled - normed * mean)).astype(BF16)

    return pl.pallas_call(
        kernel,
        out_shape=jax.ShapeDtypeStruct((1, enc, width), BF16),
        compiler_params=pltpu.CompilerParams(vmem_limit_bytes=PACK_VMEM),
        name="finish",
    )(own, *received, enc_final, norm_gain.reshape(1, width))


def body(
    enc_final, norm_gain, dec_queries, out_grad, enc_keys, enc_values, key_weight, value_weight
):
    seq = lax.axis_size("seq")
    docs = lax.axis_size("dp")
    layers = dec_queries.shape[0]
    dec, enc = dec_queries.shape[2], enc_keys.shape[2]
    arrays = (dec_queries, out_grad, enc_keys, enc_values)
    chunks = plan_chunks(layers, key_weight.shape[2])
    gathered = []
    for index, chunk in enumerate(chunks):
        bufs = pack_chunk(chunk, arrays, seq)
        gathered.append([bufs[0]] + [exchange(bufs[j], "seq", seq, j) for j in range(1, seq)])
        if index == 0:
            steps = [1 << b for b in range(seq.bit_length() - 1)]
            orders = [steps, steps[::-1]]
            finals = split_final(enc_final, bufs[0])
            halves = [gather_rows(f, seq, o) for f, o in zip(finals, orders)]
    prior = ready = None
    for index in range(len(chunks)):
        last = index == len(chunks) - 1
        outs = chunk_terms(
            index, chunks, gathered[index], key_weight, value_weight,
            ready if last else None, prior, dec, enc,
        )
        prior = outs[0]
        if index == 0:
            ready = outs[-1]
    received = [exchange(outs[j], "seq", seq, j) for j in range(1, seq)]
    gain = gain_terms(
        outs, [[a for _, a in parts] for parts in halves], [row_order(o) for o in orders]
    )
    enc_grad = finish(outs[0], received, enc_final, norm_gain)
    stages = [
        (axis, size, 1 << b)
        for axis, size in (("dp", docs), ("seq", seq))
        for b in range(size.bit_length() - 1)
    ]
    for axis, size, step in stages:
        gain = gain + exchange(gain, axis, size, step)
    return (enc_grad, gain[0] / docs)


def solution(mesh):
    placed = (
        P("dp", "seq", None),
        P(),
        P(None, "dp", "seq", None),
        P(None, "dp", "seq", None),
        P(None, "dp", "seq", None),
        P(None, "dp", "seq", None),
        P(None, None, "seq"),
        P(None, None, "seq"),
    )

    def whole(*args):
        step = jax.shard_map(body, mesh=mesh, in_specs=placed, out_specs=(P("dp", "seq", None), P()), check_vma=False)
        return step(*args)

    return whole
```

```python
import jax
import jax.numpy as jnp
from jax import lax
from jax.experimental import pallas as pl
from jax.experimental.pallas import tpu as pltpu
from jax.sharding import PartitionSpec as P


HEAD_DIM = 64
LANES = 128
PROJ_BLOCK = 1024
ATTN_ROWS = 512
PACK_VMEM = 8 << 20
LAYER_VMEM = 24 << 20
SMALL_VMEM = 2 << 20
F32 = jnp.float32
BF16 = jnp.bfloat16


def xor_pairs(size, step):
    return [(i, i ^ step) for i in range(size)]


def exchange(value, axis, size, step):
    return lax.ppermute(value, axis, xor_pairs(size, step))


def plan_chunks(layers, cols):
    chunks = [(layer, 0, cols) for layer in range(layers)]
    if cols > LANES:
        chunks[-1:] = [(layers - 1, 0, cols - LANES), (layers - 1, cols - LANES, LANES)]
    return chunks


def in_hbm(arrays):
    return [pltpu.with_memory_space_constraint(a, pltpu.HBM) for a in arrays]


def pack_chunk(chunk, arrays, seq_size):
    layer, first, width = chunk
    rows = [a.shape[2] for a in arrays]
    cols = arrays[0].shape[3] // seq_size

    def kernel(q_ref, g_ref, k_ref, v_ref, *rest):
        outs, sems = rest[:seq_size], rest[seq_size]
        me = lax.axis_index("seq")
        copies = []
        for j in list(range(1, seq_size)) + [0]:
            start = pl.multiple_of((me ^ j) * cols + first, LANES)
            base = 0
            for i, ref in enumerate((q_ref, g_ref, k_ref, v_ref)):
                copies.append(
                    pltpu.make_async_copy(
                        ref.at[layer, 0, :, pl.ds(start, width)],
                        outs[j].at[pl.ds(base, rows[i]), :],
                        sems.at[j, i],
                    )
                )
                base += rows[i]
        for c in copies:
            c.start()
        for c in copies:
            c.wait()

    return pl.pallas_call(
        kernel,
        out_shape=[jax.ShapeDtypeStruct((sum(rows), width), BF16)] * seq_size,
        in_specs=[pl.BlockSpec(memory_space=pltpu.HBM)] * 4,
        out_specs=[pl.BlockSpec(memory_space=pltpu.VMEM)] * seq_size,
        scratch_shapes=[pltpu.SemaphoreType.DMA((seq_size, 4))],
        compiler_params=pltpu.CompilerParams(vmem_limit_bytes=PACK_VMEM),
    )(*in_hbm(arrays))


def attention_into(bufs, dec, enc, kv_ref):
    cols = bufs[0].shape[1]
    count = len(bufs)
    per = LANES // HEAD_DIM
    group = max(1, ATTN_ROWS // dec)
    lane_head = lax.broadcasted_iota(jnp.int32, (1, LANES), 1) // HEAD_DIM
    rows = enc * count

    def stacked(base, ls):
        whole = jnp.concatenate([b[base : base + enc, ls].astype(F32) for b in bufs], axis=0)
        parts = [jnp.where(lane_head == h, whole, 0.0) for h in range(per)]
        return jnp.concatenate(parts, axis=0).astype(BF16)

    def chosen(stack):
        out = stack[:rows]
        for h in range(1, per):
            out = jnp.where(lane_head == h, stack[h * rows : (h + 1) * rows], out)
        return out.astype(BF16)

    nt = (((1,), (1,)), ((), ()))
    nn = (((1,), (0,)), ((), ()))
    for p in range(cols // LANES):
        ls = slice(p * LANES, (p + 1) * LANES)
        keys = stacked(2 * dec, ls)
        values = stacked(2 * dec + enc, ls)
        key_sum = value_sum = None
        for first in range(0, count, group):
            some = bufs[first : first + group]
            q = jnp.concatenate([b[0:dec, ls] for b in some], axis=0)
            g = jnp.concatenate([b[dec : 2 * dec, ls] for b in some], axis=0)
            width = q.shape[0]
            s = lax.dot_general(keys, q, nt, preferred_element_type=F32).reshape(per, rows, width)
            d = lax.dot_general(values, g, nt, preferred_element_type=F32).reshape(per, rows, width)
            e = jnp.exp(s - jnp.max(s, axis=1, keepdims=True))
            w = e * (1.0 / jnp.sum(e, axis=1, keepdims=True))
            delta = jnp.sum(w * d, axis=1, keepdims=True)
            ds = (w * (d - delta)).astype(BF16).reshape(per * rows, width)
            wl = w.astype(BF16).reshape(per * rows, width)
            vg = lax.dot_general(wl, g, nn, preferred_element_type=F32)
            kg = lax.dot_general(ds, q, nn, preferred_element_type=F32)
            key_sum = kg if key_sum is None else key_sum + kg
            value_sum = vg if value_sum is None else value_sum + vg
        kv_ref[:, ls] = chosen(key_sum)
        kv_ref[:, cols + p * LANES : cols + (p + 1) * LANES] = chosen(value_sum)


def weight_copies(chunk, key_weight, value_weight, dest, sems):
    layer, first, cols = chunk
    copies = []
    for b in range(dest.shape[0] // PROJ_BLOCK):
        rows = pl.ds(b * PROJ_BLOCK, PROJ_BLOCK)
        copies.append(
            [
                pltpu.make_async_copy(
                    src.at[layer, rows, pl.ds(first, cols)],
                    dest.at[rows, pl.ds(i * cols, cols)],
                    sems.at[b, i],
                )
                for i, src in enumerate((key_weight, value_weight))
            ]
        )
    return copies


def load_weights(chunks, key_weight, value_weight, after):
    width = key_weight.shape[1]

    def kernel(kw, vw, after_ref, *rest):
        outs, sems = rest[: len(chunks)], rest[len(chunks) :]
        copies = []
        for chunk, out, sem in zip(chunks, outs, sems):
            copies += sum(weight_copies(chunk, kw, vw, out, sem), [])
        for c in copies:
            c.start()
        for c in copies:
            c.wait()

    return pl.pallas_call(
        kernel,
        out_shape=[jax.ShapeDtypeStruct((width, 2 * cols), BF16) for _, _, cols in chunks],
        in_specs=[pl.BlockSpec(memory_space=pltpu.HBM)] * 2 + [pl.BlockSpec(memory_space=pl.ANY)],
        out_specs=[pl.BlockSpec(memory_space=pltpu.VMEM)] * len(chunks),
        scratch_shapes=[pltpu.SemaphoreType.DMA((width // PROJ_BLOCK, 2)) for _ in chunks],
        compiler_params=pltpu.CompilerParams(vmem_limit_bytes=PACK_VMEM),
        name="load_weights",
    )(*in_hbm([key_weight, value_weight]), after)


def chunk_terms(index, chunks, bufs, key_weight, value_weight, ready, prior, dec, enc):
    count = len(bufs)
    width = key_weight.shape[1]
    rows = enc * count
    nblocks = width // PROJ_BLOCK
    cols = chunks[index][2]
    last = index == len(chunks) - 1

    def kernel(*refs):
        refs = list(refs)
        buf_refs = [refs.pop(0) for _ in range(count)]
        if ready is None:
            kw, vw = refs.pop(0), refs.pop(0)
        else:
            w_ref = refs.pop(0)
        prior_ref = None if prior is None else refs.pop(0)
        outs = [refs.pop(0) for _ in range(count if last else 1)]
        kv_ref = refs.pop(0)
        if ready is None:
            w_ref, sems = refs.pop(0), refs.pop(0)
            copies = weight_copies(chunks[index], kw, vw, w_ref, sems)
            for pair in copies:
                for c in pair:
                    c.start()
        attention_into(buf_refs, dec, enc, kv_ref)
        nt = (((1,), (1,)), ((), ()))
        for b in range(nblocks):
            bs = slice(b * PROJ_BLOCK, (b + 1) * PROJ_BLOCK)
            if ready is None:
                for c in copies[b]:
                    c.wait()
            acc = lax.dot_general(kv_ref[...], w_ref[bs, :], nt, preferred_element_type=F32)
            if prior is not None:
                acc += prior_ref[:, bs]
            if last:
                for j in range(count):
                    outs[j][:, bs] = acc[j * enc : (j + 1) * enc].astype(outs[j].dtype)
            else:
                outs[0][:, bs] = acc

    if last:
        out_shape = [jax.ShapeDtypeStruct((enc, width), F32 if j == 0 else BF16) for j in range(count)]
    else:
        out_shape = [jax.ShapeDtypeStruct((rows, width), F32)]
    scratch = [pltpu.VMEM((rows, 2 * cols), BF16)]
    if ready is None:
        scratch += [pltpu.VMEM((width, 2 * cols), BF16), pltpu.SemaphoreType.DMA((nblocks, 2))]
    vmem = pl.BlockSpec(memory_space=pltpu.VMEM)
    if ready is None:
        weights, specs = in_hbm([key_weight, value_weight]), [pl.BlockSpec(memory_space=pltpu.HBM)] * 2
    else:
        weights, specs = [ready], [vmem]
    tail = [] if prior is None else [prior]
    return pl.pallas_call(
        kernel,
        out_shape=out_shape,
        in_specs=[vmem] * count + specs + [vmem] * len(tail),
        out_specs=[vmem] * len(out_shape),
        scratch_shapes=scratch,
        compiler_params=pltpu.CompilerParams(vmem_limit_bytes=LAYER_VMEM),
    )(*bufs, *weights, *tail)


def split_final(enc_final, after):
    enc, half = enc_final.shape[1], enc_final.shape[2] // 2

    def kernel(src, after_ref, *rest):
        outs, sems = rest[:2], rest[2]
        copies = [
            pltpu.make_async_copy(src.at[0, :, pl.ds(h * half, half)], outs[h], sems.at[h])
            for h in range(2)
        ]
        for c in copies:
            c.start()
        for c in copies:
            c.wait()

    return pl.pallas_call(
        kernel,
        out_shape=[jax.ShapeDtypeStruct((enc, half), BF16)] * 2,
        in_specs=[pl.BlockSpec(memory_space=pltpu.HBM), pl.BlockSpec(memory_space=pl.ANY)],
        out_specs=[pl.BlockSpec(memory_space=pltpu.VMEM)] * 2,
        scratch_shapes=[pltpu.SemaphoreType.DMA((2,))],
        compiler_params=pltpu.CompilerParams(vmem_limit_bytes=SMALL_VMEM),
        name="split_final",
    )(*in_hbm([enc_final]), after)


def gather_rows(mine, seq_size, steps):
    have = [(0, mine)]
    for n, step in enumerate(steps):
        whole = have[0][1] if n == 0 else jnp.concatenate([a for _, a in have], axis=0)
        have = have + [(step, exchange(whole, "seq", seq_size, step))]
    return have


def row_order(steps):
    order = [0]
    for step in steps:
        order = order + [j ^ step for j in order]
    return order


def gain_terms(pieces, halves, orders):
    count = len(pieces)
    enc, width = pieces[0].shape
    half = width // 2
    sizes = [len(parts) for parts in halves]

    def kernel(*refs):
        piece_refs = refs[:count]
        part_refs = [refs[count : count + sizes[0]], refs[count + sizes[0] : count + sum(sizes)]]
        out_ref = refs[-1]
        blocks = [[None] * count, [None] * count]
        for h in range(2):
            place = 0
            for ref in part_refs[h]:
                for k in range(ref.shape[0] // enc):
                    blocks[h][orders[h][place]] = (ref, k * enc)
                    place += 1
        inv = []
        for j in range(count):
            square = None
            for h in range(2):
                ref, base = blocks[h][j]
                x = ref[pl.ds(base, enc), :].astype(F32)
                total = jnp.sum(x * x, axis=-1, keepdims=True)
                square = total if square is None else square + total
            inv.append(lax.rsqrt(square * (1.0 / width) + 1e-06))
        for h in range(2):
            hs = slice(h * half, (h + 1) * half)
            terms = None
            for j in range(count):
                ref, base = blocks[h][j]
                normed = ref[pl.ds(base, enc), :].astype(F32) * inv[j]
                product = piece_refs[j][:, hs].astype(F32) * normed
                terms = product if terms is None else terms + product
            out_ref[:, hs] = jnp.sum(terms, axis=0, keepdims=True)

    return pl.pallas_call(
        kernel,
        out_shape=jax.ShapeDtypeStruct((1, width), F32),
        compiler_params=pltpu.CompilerParams(vmem_limit_bytes=PACK_VMEM),
        name="gain_terms",
    )(*pieces, *[a for parts in halves for a in parts])


def finish(own, received, enc_final, norm_gain):
    enc, width = own.shape

    def kernel(own_ref, *refs):
        recv_refs = refs[: len(received)]
        final_ref, gain_ref, grad_ref = refs[len(received) :]
        state = own_ref[...]
        for r in recv_refs:
            state = state + r[...].astype(F32)
        final = final_ref[0].astype(F32)
        inv_rms = lax.rsqrt(jnp.mean(final * final, axis=-1, keepdims=True) + 1e-06)
        normed = final * inv_rms
        scaled = gain_ref[...] * state
        mean = jnp.mean(scaled * normed, axis=-1, keepdims=True)
        grad_ref[0] = (inv_rms * (scaled - normed * mean)).astype(BF16)

    return pl.pallas_call(
        kernel,
        out_shape=jax.ShapeDtypeStruct((1, enc, width), BF16),
        compiler_params=pltpu.CompilerParams(vmem_limit_bytes=PACK_VMEM),
        name="finish",
    )(own, *received, enc_final, norm_gain.reshape(1, width))


def body(
    enc_final, norm_gain, dec_queries, out_grad, enc_keys, enc_values, key_weight, value_weight
):
    seq = lax.axis_size("seq")
    docs = lax.axis_size("dp")
    layers = dec_queries.shape[0]
    dec, enc = dec_queries.shape[2], enc_keys.shape[2]
    arrays = (dec_queries, out_grad, enc_keys, enc_values)
    chunks = plan_chunks(layers, key_weight.shape[2])
    gathered = []
    for index, chunk in enumerate(chunks):
        bufs = pack_chunk(chunk, arrays, seq)
        gathered.append([bufs[0]] + [exchange(bufs[j], "seq", seq, j) for j in range(1, seq)])
        if index == 0:
            steps = [1 << b for b in range(seq.bit_length() - 1)]
            orders = [steps, steps[::-1]]
            finals = split_final(enc_final, bufs[0])
            halves = [gather_rows(f, seq, o) for f, o in zip(finals, orders)]
    ready = load_weights(chunks[1:], key_weight, value_weight, gathered[-1][0])
    prior = None
    for index in range(len(chunks)):
        outs = chunk_terms(
            index, chunks, gathered[index], key_weight, value_weight,
            ready[index - 1] if index else None, prior, dec, enc,
        )
        prior = outs[0]
    received = [exchange(outs[j], "seq", seq, j) for j in range(1, seq)]
    gain = gain_terms(
        outs, [[a for _, a in parts] for parts in halves], [row_order(o) for o in orders]
    )
    enc_grad = finish(outs[0], received, enc_final, norm_gain)
    stages = [
        (axis, size, 1 << b)
        for axis, size in (("dp", docs), ("seq", seq))
        for b in range(size.bit_length() - 1)
    ]
    for axis, size, step in stages:
        gain = gain + exchange(gain, axis, size, step)
    return (enc_grad, gain[0] / docs)


def solution(mesh):
    placed = (
        P("dp", "seq", None),
        P(),
        P(None, "dp", "seq", None),
        P(None, "dp", "seq", None),
        P(None, "dp", "seq", None),
        P(None, "dp", "seq", None),
        P(None, None, "seq"),
        P(None, None, "seq"),
    )

    def whole(*args):
        step = jax.shard_map(body, mesh=mesh, in_specs=placed, out_specs=(P("dp", "seq", None), P()), check_vma=False)
        return step(*args)

    return whole
```

```python
import jax
import jax.numpy as jnp
from jax import lax
from jax.experimental import pallas as pl
from jax.experimental.pallas import tpu as pltpu
from jax.sharding import PartitionSpec as P


HEAD_DIM = 64
LANES = 128
PROJ_BLOCK = 1024
ATTN_ROWS = 512
PACK_VMEM = 8 << 20
LAYER_VMEM = 24 << 20
F32 = jnp.float32
BF16 = jnp.bfloat16


def xor_pairs(size, step):
    return [(i, i ^ step) for i in range(size)]


def exchange(value, axis, size, step):
    return lax.ppermute(value, axis, xor_pairs(size, step))


def plan_chunks(layers, cols):
    chunks = [(layer, 0, cols) for layer in range(layers)]
    if cols > LANES:
        chunks[-1:] = [(layers - 1, 0, cols - LANES), (layers - 1, cols - LANES, LANES)]
    return chunks


def in_hbm(arrays):
    return [pltpu.with_memory_space_constraint(a, pltpu.HBM) for a in arrays]


def pack_chunk(chunk, arrays, seq_size):
    layer, first, width = chunk
    rows = [a.shape[2] for a in arrays]
    cols = arrays[0].shape[3] // seq_size

    def kernel(q_ref, g_ref, k_ref, v_ref, *rest):
        outs, sems = rest[:seq_size], rest[seq_size]
        me = lax.axis_index("seq")
        copies = []
        for j in list(range(1, seq_size)) + [0]:
            start = pl.multiple_of((me ^ j) * cols + first, LANES)
            base = 0
            for i, ref in enumerate((q_ref, g_ref, k_ref, v_ref)):
                copies.append(
                    pltpu.make_async_copy(
                        ref.at[layer, 0, :, pl.ds(start, width)],
                        outs[j].at[pl.ds(base, rows[i]), :],
                        sems.at[j, i],
                    )
                )
                base += rows[i]
        for c in copies:
            c.start()
        for c in copies:
            c.wait()

    return pl.pallas_call(
        kernel,
        out_shape=[jax.ShapeDtypeStruct((sum(rows), width), BF16)] * seq_size,
        in_specs=[pl.BlockSpec(memory_space=pltpu.HBM)] * 4,
        out_specs=[pl.BlockSpec(memory_space=pltpu.VMEM)] * seq_size,
        scratch_shapes=[pltpu.SemaphoreType.DMA((seq_size, 4))],
        compiler_params=pltpu.CompilerParams(vmem_limit_bytes=PACK_VMEM),
    )(*in_hbm(arrays))


def attention_into(bufs, dec, enc, kv_ref):
    cols = bufs[0].shape[1]
    count = len(bufs)
    per = LANES // HEAD_DIM
    group = max(1, ATTN_ROWS // dec)
    lane_head = lax.broadcasted_iota(jnp.int32, (1, LANES), 1) // HEAD_DIM
    rows = enc * count

    def stacked(base, ls):
        whole = jnp.concatenate([b[base : base + enc, ls].astype(F32) for b in bufs], axis=0)
        parts = [jnp.where(lane_head == h, whole, 0.0) for h in range(per)]
        return jnp.concatenate(parts, axis=0).astype(BF16)

    def chosen(stack):
        out = stack[:rows]
        for h in range(1, per):
            out = jnp.where(lane_head == h, stack[h * rows : (h + 1) * rows], out)
        return out.astype(BF16)

    nt = (((1,), (1,)), ((), ()))
    nn = (((1,), (0,)), ((), ()))
    for p in range(cols // LANES):
        ls = slice(p * LANES, (p + 1) * LANES)
        keys = stacked(2 * dec, ls)
        values = stacked(2 * dec + enc, ls)
        key_sum = value_sum = None
        for first in range(0, count, group):
            some = bufs[first : first + group]
            q = jnp.concatenate([b[0:dec, ls] for b in some], axis=0)
            g = jnp.concatenate([b[dec : 2 * dec, ls] for b in some], axis=0)
            width = q.shape[0]
            s = lax.dot_general(keys, q, nt, preferred_element_type=F32).reshape(per, rows, width)
            d = lax.dot_general(values, g, nt, preferred_element_type=F32).reshape(per, rows, width)
            e = jnp.exp(s - jnp.max(s, axis=1, keepdims=True))
            w = e * (1.0 / jnp.sum(e, axis=1, keepdims=True))
            delta = jnp.sum(w * d, axis=1, keepdims=True)
            ds = (w * (d - delta)).astype(BF16).reshape(per * rows, width)
            wl = w.astype(BF16).reshape(per * rows, width)
            vg = lax.dot_general(wl, g, nn, preferred_element_type=F32)
            kg = lax.dot_general(ds, q, nn, preferred_element_type=F32)
            key_sum = kg if key_sum is None else key_sum + kg
            value_sum = vg if value_sum is None else value_sum + vg
        kv_ref[:, ls] = chosen(key_sum)
        kv_ref[:, cols + p * LANES : cols + (p + 1) * LANES] = chosen(value_sum)


def weight_copies(chunk, key_weight, value_weight, dest, sems):
    layer, first, cols = chunk
    copies = []
    for b in range(dest.shape[0] // PROJ_BLOCK):
        rows = pl.ds(b * PROJ_BLOCK, PROJ_BLOCK)
        copies.append(
            [
                pltpu.make_async_copy(
                    src.at[layer, rows, pl.ds(first, cols)],
                    dest.at[rows, pl.ds(i * cols, cols)],
                    sems.at[b, i],
                )
                for i, src in enumerate((key_weight, value_weight))
            ]
        )
    return copies


def load_weights(chunks, key_weight, value_weight, after):
    width = key_weight.shape[1]

    def kernel(kw, vw, after_ref, *rest):
        outs, sems = rest[: len(chunks)], rest[len(chunks) :]
        copies = []
        for chunk, out, sem in zip(chunks, outs, sems):
            copies += sum(weight_copies(chunk, kw, vw, out, sem), [])
        for c in copies:
            c.start()
        for c in copies:
            c.wait()

    return pl.pallas_call(
        kernel,
        out_shape=[jax.ShapeDtypeStruct((width, 2 * cols), BF16) for _, _, cols in chunks],
        in_specs=[pl.BlockSpec(memory_space=pltpu.HBM)] * 2 + [pl.BlockSpec(memory_space=pl.ANY)],
        out_specs=[pl.BlockSpec(memory_space=pltpu.VMEM)] * len(chunks),
        scratch_shapes=[pltpu.SemaphoreType.DMA((width // PROJ_BLOCK, 2)) for _ in chunks],
        compiler_params=pltpu.CompilerParams(vmem_limit_bytes=PACK_VMEM),
        name="load_weights",
    )(*in_hbm([key_weight, value_weight]), after)


def chunk_terms(index, chunks, bufs, key_weight, value_weight, ready, prior, dec, enc):
    count = len(bufs)
    width = key_weight.shape[1]
    rows = enc * count
    nblocks = width // PROJ_BLOCK
    cols = chunks[index][2]
    last = index == len(chunks) - 1

    def kernel(*refs):
        refs = list(refs)
        buf_refs = [refs.pop(0) for _ in range(count)]
        if ready is None:
            kw, vw = refs.pop(0), refs.pop(0)
        else:
            w_ref = refs.pop(0)
        prior_ref = None if prior is None else refs.pop(0)
        outs = [refs.pop(0) for _ in range(count if last else 1)]
        kv_ref = refs.pop(0)
        if ready is None:
            w_ref, sems = refs.pop(0), refs.pop(0)
            copies = weight_copies(chunks[index], kw, vw, w_ref, sems)
            for pair in copies:
                for c in pair:
                    c.start()
        attention_into(buf_refs, dec, enc, kv_ref)
        nt = (((1,), (1,)), ((), ()))
        for b in range(nblocks):
            bs = slice(b * PROJ_BLOCK, (b + 1) * PROJ_BLOCK)
            if ready is None:
                for c in copies[b]:
                    c.wait()
            acc = lax.dot_general(kv_ref[...], w_ref[bs, :], nt, preferred_element_type=F32)
            if prior is not None:
                acc += prior_ref[:, bs]
            if last:
                for j in range(count):
                    outs[j][:, bs] = acc[j * enc : (j + 1) * enc].astype(outs[j].dtype)
            else:
                outs[0][:, bs] = acc

    if last:
        out_shape = [jax.ShapeDtypeStruct((enc, width), F32 if j == 0 else BF16) for j in range(count)]
    else:
        out_shape = [jax.ShapeDtypeStruct((rows, width), F32)]
    scratch = [pltpu.VMEM((rows, 2 * cols), BF16)]
    if ready is None:
        scratch += [pltpu.VMEM((width, 2 * cols), BF16), pltpu.SemaphoreType.DMA((nblocks, 2))]
    vmem = pl.BlockSpec(memory_space=pltpu.VMEM)
    if ready is None:
        weights, specs = in_hbm([key_weight, value_weight]), [pl.BlockSpec(memory_space=pltpu.HBM)] * 2
    else:
        weights, specs = [ready], [vmem]
    tail = [] if prior is None else [prior]
    return pl.pallas_call(
        kernel,
        out_shape=out_shape,
        in_specs=[vmem] * count + specs + [vmem] * len(tail),
        out_specs=[vmem] * len(out_shape),
        scratch_shapes=scratch,
        compiler_params=pltpu.CompilerParams(vmem_limit_bytes=LAYER_VMEM),
    )(*bufs, *weights, *tail)


def gather_rows(enc_final, seq_size):
    enc, width = enc_final.shape[1], enc_final.shape[2]
    rows = {0: [(enc_final, 0, 0, width)]}
    if seq_size == 4:
        half = width // 2
        near = {j: exchange(enc_final, "seq", seq_size, j) for j in (1, 2)}
        for j in (1, 2):
            rows[j] = [(near[j], 0, 0, width)]
        sends = [near[1][:, :, :half], near[2][:, :, half:]]
        low = exchange(sends[0], "seq", seq_size, 2)
        high = exchange(sends[1], "seq", seq_size, 1)
        rows[3] = [(low, 0, 0, half), (high, 0, half, half)]
        return rows
    have, order = [enc_final], [0]
    step = 1
    while step < seq_size:
        whole = jnp.concatenate(have, axis=1) if len(have) > 1 else have[0]
        got = exchange(whole, "seq", seq_size, step)
        for place, j in enumerate(order):
            rows[j ^ step] = [(got, place * enc, 0, width)]
        have, order = have + [got], order + [j ^ step for j in order]
        step *= 2
    return rows


def gain_terms(pieces, rows):
    count = len(pieces)
    enc, width = pieces[0].shape
    arrays = []
    places = []
    for j in range(count):
        spots = []
        for array, base, first, cols in rows[j]:
            known = [n for n, a in enumerate(arrays) if a is array]
            if not known:
                arrays.append(array)
                known = [len(arrays) - 1]
            spots.append((known[0], base, first, cols))
        places.append(spots)
    cuts = sorted({first for spots in places for _, _, first, _ in spots} | {width})

    def kernel(*refs):
        piece_refs, row_refs, out_ref = refs[:count], refs[count:-1], refs[-1]
        inv = []
        for spots in places:
            square = 0.0
            for n, base, _, cols in spots:
                x = row_refs[n][0, pl.ds(base, enc), :].astype(F32)
                square = square + jnp.sum(x * x, axis=-1, keepdims=True)
            inv.append(lax.rsqrt(square * (1.0 / width) + 1e-06))
        for low, high in zip(cuts[:-1], cuts[1:]):
            terms = None
            for j, spots in enumerate(places):
                for n, base, first, cols in spots:
                    if first <= low and high <= first + cols:
                        x = row_refs[n][0, pl.ds(base, enc), pl.ds(low - first, high - low)]
                        product = piece_refs[j][:, low:high].astype(F32) * (x.astype(F32) * inv[j])
                        terms = product if terms is None else terms + product
            out_ref[:, low:high] = jnp.sum(terms, axis=0, keepdims=True)

    return pl.pallas_call(
        kernel,
        out_shape=jax.ShapeDtypeStruct((1, width), F32),
        compiler_params=pltpu.CompilerParams(vmem_limit_bytes=PACK_VMEM),
        name="gain_terms",
    )(*pieces, *arrays)


def finish(own, received, enc_final, norm_gain):
    enc, width = own.shape

    def kernel(own_ref, *refs):
        recv_refs = refs[: len(received)]
        final_ref, gain_ref, grad_ref = refs[len(received) :]
        state = own_ref[...]
        for r in recv_refs:
            state = state + r[...].astype(F32)
        final = final_ref[0].astype(F32)
        inv_rms = lax.rsqrt(jnp.mean(final * final, axis=-1, keepdims=True) + 1e-06)
        normed = final * inv_rms
        scaled = gain_ref[...] * state
        mean = jnp.mean(scaled * normed, axis=-1, keepdims=True)
        grad_ref[0] = (inv_rms * (scaled - normed * mean)).astype(BF16)

    return pl.pallas_call(
        kernel,
        out_shape=jax.ShapeDtypeStruct((1, enc, width), BF16),
        compiler_params=pltpu.CompilerParams(vmem_limit_bytes=PACK_VMEM),
        name="finish",
    )(own, *received, enc_final, norm_gain.reshape(1, width))


def body(
    enc_final, norm_gain, dec_queries, out_grad, enc_keys, enc_values, key_weight, value_weight
):
    seq = lax.axis_size("seq")
    docs = lax.axis_size("dp")
    layers = dec_queries.shape[0]
    dec, enc = dec_queries.shape[2], enc_keys.shape[2]
    arrays = (dec_queries, out_grad, enc_keys, enc_values)
    chunks = plan_chunks(layers, key_weight.shape[2])
    rows = gather_rows(enc_final, seq)
    gathered = []
    for chunk in chunks:
        bufs = pack_chunk(chunk, arrays, seq)
        moved = [bufs[0]]
        for j in range(1, seq):
            moved.append(exchange(bufs[j], "seq", seq, j))
        gathered.append(moved)
    ready = load_weights(chunks[1:], key_weight, value_weight, gathered[-1][0])
    prior = None
    for index in range(len(chunks)):
        outs = chunk_terms(
            index, chunks, gathered[index], key_weight, value_weight,
            ready[index - 1] if index else None, prior, dec, enc,
        )
        prior = outs[0]
    received = [exchange(outs[j], "seq", seq, j) for j in range(1, seq)]
    gain = gain_terms(outs, rows)
    enc_grad = finish(outs[0], received, enc_final, norm_gain)
    stages = [
        (axis, size, 1 << b)
        for axis, size in (("dp", docs), ("seq", seq))
        for b in range(size.bit_length() - 1)
    ]
    for axis, size, step in stages:
        gain = gain + exchange(gain, axis, size, step)
    return (enc_grad, gain[0] / docs)


def solution(mesh):
    placed = (
        P("dp", "seq", None),
        P(),
        P(None, "dp", "seq", None),
        P(None, "dp", "seq", None),
        P(None, "dp", "seq", None),
        P(None, "dp", "seq", None),
        P(None, None, "seq"),
        P(None, None, "seq"),
    )

    def whole(*args):
        step = jax.shard_map(body, mesh=mesh, in_specs=placed, out_specs=(P("dp", "seq", None), P()), check_vma=False)
        return step(*args)

    return whole
```

```python
import jax
import jax.numpy as jnp
from jax import lax
from jax.experimental import pallas as pl
from jax.experimental.pallas import tpu as pltpu
from jax.sharding import PartitionSpec as P


HEAD_DIM = 64
LANES = 128
PROJ_BLOCK = 1024
TAIL_PAIRS = (2, 1)
ATTN_ROWS = 512
PACK_VMEM = 8 << 20
LAYER_VMEM = 20 << 20
F32 = jnp.float32
BF16 = jnp.bfloat16


def xor_pairs(size, step):
    return [(i, i ^ step) for i in range(size)]


def exchange(value, axis, size, step):
    return lax.ppermute(value, axis, xor_pairs(size, step))


def plan_chunks(layers, cols):
    pairs = [(layer, first) for layer in range(layers) for first in range(0, cols, LANES)]
    tail = [n for n in TAIL_PAIRS if len(pairs) >= 2 * sum(TAIL_PAIRS)] or [1]
    cuts = [0, len(pairs) - sum(tail)]
    for n in tail:
        cuts.append(cuts[-1] + n)
    chunks = []
    for low, high in zip(cuts[:-1], cuts[1:]):
        chunk = []
        for layer, first in pairs[low:high]:
            if chunk and chunk[-1][0] == layer:
                chunk[-1] = (layer, chunk[-1][1], chunk[-1][2] + LANES)
            else:
                chunk.append((layer, first, LANES))
        chunks.append(chunk)
    return chunks


def chunk_width(chunk):
    return sum(width for _, _, width in chunk)


def in_hbm(arrays):
    return [pltpu.with_memory_space_constraint(a, pltpu.HBM) for a in arrays]


def pack_chunk(chunk, arrays, seq_size):
    width = chunk_width(chunk)
    rows = [a.shape[2] for a in arrays]
    cols = arrays[0].shape[3] // seq_size

    def kernel(q_ref, g_ref, k_ref, v_ref, *rest):
        outs, sems = rest[:seq_size], rest[seq_size]
        me = lax.axis_index("seq")
        copies = []
        for j in list(range(1, seq_size)) + [0]:
            left = 0
            for n, (layer, first, part) in enumerate(chunk):
                start = pl.multiple_of((me ^ j) * cols + first, LANES)
                base = 0
                for i, ref in enumerate((q_ref, g_ref, k_ref, v_ref)):
                    copies.append(
                        pltpu.make_async_copy(
                            ref.at[layer, 0, :, pl.ds(start, part)],
                            outs[j].at[pl.ds(base, rows[i]), pl.ds(left, part)],
                            sems.at[j, n, i],
                        )
                    )
                    base += rows[i]
                left += part
        for c in copies:
            c.start()
        for c in copies:
            c.wait()

    return pl.pallas_call(
        kernel,
        out_shape=[jax.ShapeDtypeStruct((sum(rows), width), BF16)] * seq_size,
        in_specs=[pl.BlockSpec(memory_space=pltpu.HBM)] * 4,
        out_specs=[pl.BlockSpec(memory_space=pltpu.VMEM)] * seq_size,
        scratch_shapes=[pltpu.SemaphoreType.DMA((seq_size, len(chunk), 4))],
        compiler_params=pltpu.CompilerParams(vmem_limit_bytes=PACK_VMEM),
    )(*in_hbm(arrays))


def attention_into(bufs, dec, enc, kv_ref):
    cols = bufs[0].shape[1]
    count = len(bufs)
    per = LANES // HEAD_DIM
    group = max(1, ATTN_ROWS // dec)
    lane_head = lax.broadcasted_iota(jnp.int32, (1, LANES), 1) // HEAD_DIM
    rows = enc * count

    def stacked(base, ls):
        whole = jnp.concatenate([b[base : base + enc, ls].astype(F32) for b in bufs], axis=0)
        parts = [jnp.where(lane_head == h, whole, 0.0) for h in range(per)]
        return jnp.concatenate(parts, axis=0).astype(BF16)

    def chosen(stack):
        out = stack[:rows]
        for h in range(1, per):
            out = jnp.where(lane_head == h, stack[h * rows : (h + 1) * rows], out)
        return out.astype(BF16)

    nt = (((1,), (1,)), ((), ()))
    nn = (((1,), (0,)), ((), ()))
    for p in range(cols // LANES):
        ls = slice(p * LANES, (p + 1) * LANES)
        keys = stacked(2 * dec, ls)
        values = stacked(2 * dec + enc, ls)
        key_sum = value_sum = None
        for first in range(0, count, group):
            some = bufs[first : first + group]
            q = jnp.concatenate([b[0:dec, ls] for b in some], axis=0)
            g = jnp.concatenate([b[dec : 2 * dec, ls] for b in some], axis=0)
            width = q.shape[0]
            s = lax.dot_general(keys, q, nt, preferred_element_type=F32).reshape(per, rows, width)
            d = lax.dot_general(values, g, nt, preferred_element_type=F32).reshape(per, rows, width)
            e = jnp.exp(s - jnp.max(s, axis=1, keepdims=True))
            w = e * (1.0 / jnp.sum(e, axis=1, keepdims=True))
            delta = jnp.sum(w * d, axis=1, keepdims=True)
            ds = (w * (d - delta)).astype(BF16).reshape(per * rows, width)
            wl = w.astype(BF16).reshape(per * rows, width)
            vg = lax.dot_general(wl, g, nn, preferred_element_type=F32)
            kg = lax.dot_general(ds, q, nn, preferred_element_type=F32)
            key_sum = kg if key_sum is None else key_sum + kg
            value_sum = vg if value_sum is None else value_sum + vg
        kv_ref[:, ls] = chosen(key_sum)
        kv_ref[:, cols + p * LANES : cols + (p + 1) * LANES] = chosen(value_sum)


def weight_copies(chunk, key_weight, value_weight, dest, sems):
    copies = []
    left = 0
    for n, (layer, first, part) in enumerate(chunk):
        for i, src in enumerate((key_weight, value_weight)):
            copies.append(
                pltpu.make_async_copy(
                    src.at[layer, :, pl.ds(first, part)],
                    dest.at[:, pl.ds(i * chunk_width(chunk) + left, part)],
                    sems.at[n, i],
                )
            )
        left += part
    return copies


def load_weights(chunks, key_weight, value_weight, after):
    width = key_weight.shape[1]

    def kernel(kw, vw, after_ref, *rest):
        outs, sems = rest[: len(chunks)], rest[len(chunks) :]
        copies = []
        for chunk, out, sem in zip(chunks, outs, sems):
            copies += weight_copies(chunk, kw, vw, out, sem)
        for c in copies:
            c.start()
        for c in copies:
            c.wait()

    return pl.pallas_call(
        kernel,
        out_shape=[jax.ShapeDtypeStruct((width, 2 * chunk_width(c)), BF16) for c in chunks],
        in_specs=[pl.BlockSpec(memory_space=pltpu.HBM)] * 2 + [pl.BlockSpec(memory_space=pl.ANY)],
        out_specs=[pl.BlockSpec(memory_space=pltpu.VMEM)] * len(chunks),
        scratch_shapes=[pltpu.SemaphoreType.DMA((len(c), 2)) for c in chunks],
        compiler_params=pltpu.CompilerParams(vmem_limit_bytes=PACK_VMEM),
        name="load_weights",
    )(*in_hbm([key_weight, value_weight]), after)


def chunk_terms(bufs, weight, prior, dec, enc, last):
    count = len(bufs)
    width = weight.shape[0]
    rows = enc * count

    def kernel(*refs):
        buf_refs, w_ref, kv_ref = refs[:count], refs[count], refs[-1]
        prior_ref = None if prior is None else refs[count + 1]
        outs = refs[count + 1 + (prior is not None) : -1]
        attention_into(buf_refs, dec, enc, kv_ref)
        nt = (((1,), (1,)), ((), ()))
        for b in range(width // PROJ_BLOCK):
            bs = slice(b * PROJ_BLOCK, (b + 1) * PROJ_BLOCK)
            acc = lax.dot_general(kv_ref[...], w_ref[bs, :], nt, preferred_element_type=F32)
            if prior is not None:
                acc += prior_ref[:, bs]
            if last:
                for j in range(count):
                    outs[j][:, bs] = acc[j * enc : (j + 1) * enc].astype(outs[j].dtype)
            else:
                outs[0][:, bs] = acc

    if last:
        out_shape = [jax.ShapeDtypeStruct((enc, width), F32 if j == 0 else BF16) for j in range(count)]
    else:
        out_shape = [jax.ShapeDtypeStruct((rows, width), F32)]
    vmem = pl.BlockSpec(memory_space=pltpu.VMEM)
    operands = list(bufs) + [weight] + ([] if prior is None else [prior])
    return pl.pallas_call(
        kernel,
        out_shape=out_shape,
        in_specs=[vmem] * len(operands),
        out_specs=[vmem] * len(out_shape),
        scratch_shapes=[pltpu.VMEM((rows, weight.shape[1]), BF16)],
        compiler_params=pltpu.CompilerParams(vmem_limit_bytes=LAYER_VMEM),
    )(*operands)


def gather_rows(enc_final, seq_size):
    enc, width = enc_final.shape[1], enc_final.shape[2]
    rows = {0: [(enc_final, 0, 0, width)]}
    if seq_size == 4:
        half = width // 2 // LANES * LANES
        near = {j: exchange(enc_final, "seq", seq_size, j) for j in (1, 2)}
        for j in (1, 2):
            rows[j] = [(near[j], 0, 0, width)]
        sends = [near[1][:, :, :half], near[2][:, :, half:]]
        low = exchange(sends[0], "seq", seq_size, 2)
        high = exchange(sends[1], "seq", seq_size, 1)
        rows[3] = [(low, 0, 0, half), (high, 0, half, width - half)]
        return rows
    have, order = [enc_final], [0]
    step = 1
    while step < seq_size:
        whole = jnp.concatenate(have, axis=1) if len(have) > 1 else have[0]
        got = exchange(whole, "seq", seq_size, step)
        for place, j in enumerate(order):
            rows[j ^ step] = [(got, place * enc, 0, width)]
        have, order = have + [got], order + [j ^ step for j in order]
        step *= 2
    return rows


def gain_terms(pieces, rows):
    count = len(pieces)
    enc, width = pieces[0].shape
    arrays = []
    places = []
    for j in range(count):
        spots = []
        for array, base, first, cols in rows[j]:
            known = [n for n, a in enumerate(arrays) if a is array]
            if not known:
                arrays.append(array)
                known = [len(arrays) - 1]
            spots.append((known[0], base, first, cols))
        places.append(spots)
    cuts = sorted({first for spots in places for _, _, first, _ in spots} | {width})

    def kernel(*refs):
        piece_refs, row_refs, out_ref = refs[:count], refs[count:-1], refs[-1]
        inv = []
        for spots in places:
            square = 0.0
            for n, base, _, cols in spots:
                x = row_refs[n][0, pl.ds(base, enc), :].astype(F32)
                square = square + jnp.sum(x * x, axis=-1, keepdims=True)
            inv.append(lax.rsqrt(square * (1.0 / width) + 1e-06))
        for low, high in zip(cuts[:-1], cuts[1:]):
            terms = None
            for j, spots in enumerate(places):
                for n, base, first, cols in spots:
                    if first <= low and high <= first + cols:
                        x = row_refs[n][0, pl.ds(base, enc), pl.ds(low - first, high - low)]
                        product = piece_refs[j][:, low:high].astype(F32) * (x.astype(F32) * inv[j])
                        terms = product if terms is None else terms + product
            out_ref[:, low:high] = jnp.sum(terms, axis=0, keepdims=True)

    return pl.pallas_call(
        kernel,
        out_shape=jax.ShapeDtypeStruct((1, width), F32),
        compiler_params=pltpu.CompilerParams(vmem_limit_bytes=PACK_VMEM),
        name="gain_terms",
    )(*pieces, *arrays)


def finish(own, received, enc_final, norm_gain):
    enc, width = own.shape

    def kernel(own_ref, *refs):
        recv_refs = refs[: len(received)]
        final_ref, gain_ref, grad_ref = refs[len(received) :]
        state = own_ref[...]
        for r in recv_refs:
            state = state + r[...].astype(F32)
        final = final_ref[0].astype(F32)
        inv_rms = lax.rsqrt(jnp.mean(final * final, axis=-1, keepdims=True) + 1e-06)
        normed = final * inv_rms
        scaled = gain_ref[...] * state
        mean = jnp.mean(scaled * normed, axis=-1, keepdims=True)
        grad_ref[0] = (inv_rms * (scaled - normed * mean)).astype(BF16)

    return pl.pallas_call(
        kernel,
        out_shape=jax.ShapeDtypeStruct((1, enc, width), BF16),
        compiler_params=pltpu.CompilerParams(vmem_limit_bytes=PACK_VMEM),
        name="finish",
    )(own, *received, enc_final, norm_gain.reshape(1, width))


def body(
    enc_final, norm_gain, dec_queries, out_grad, enc_keys, enc_values, key_weight, value_weight
):
    seq = lax.axis_size("seq")
    docs = lax.axis_size("dp")
    layers = dec_queries.shape[0]
    dec, enc = dec_queries.shape[2], enc_keys.shape[2]
    arrays = (dec_queries, out_grad, enc_keys, enc_values)
    chunks = plan_chunks(layers, key_weight.shape[2])
    rows = gather_rows(enc_final, seq)
    gathered = []
    for chunk in chunks:
        bufs = pack_chunk(chunk, arrays, seq)
        moved = [bufs[0]]
        for j in range(1, seq):
            moved.append(exchange(bufs[j], "seq", seq, j))
        gathered.append(moved)
    weights = load_weights(chunks, key_weight, value_weight, gathered[-1][0])
    prior = None
    for index in range(len(chunks)):
        outs = chunk_terms(
            gathered[index], weights[index], prior, dec, enc, index == len(chunks) - 1
        )
        prior = outs[0]
    received = [exchange(outs[j], "seq", seq, j) for j in range(1, seq)]
    gain = gain_terms(outs, rows)
    enc_grad = finish(outs[0], received, enc_final, norm_gain)
    stages = [
        (axis, size, 1 << b)
        for axis, size in (("dp", docs), ("seq", seq))
        for b in range(size.bit_length() - 1)
    ]
    for axis, size, step in stages:
        gain = gain + exchange(gain, axis, size, step)
    return (enc_grad, gain[0] / docs)


def solution(mesh):
    placed = (
        P("dp", "seq", None),
        P(),
        P(None, "dp", "seq", None),
        P(None, "dp", "seq", None),
        P(None, "dp", "seq", None),
        P(None, "dp", "seq", None),
        P(None, None, "seq"),
        P(None, None, "seq"),
    )

    def whole(*args):
        step = jax.shard_map(
            body, mesh=mesh, in_specs=placed, out_specs=(P("dp", "seq", None), P()), check_vma=False
        )
        return step(*args)

    return whole
```

```python
import jax
import jax.numpy as jnp
from jax import lax
from jax.experimental import pallas as pl
from jax.experimental.pallas import tpu as pltpu
from jax.sharding import PartitionSpec as P


HEAD_DIM = 64
LANES = 128
PROJ_BLOCK = 2048
TAIL_PAIRS = (2, 1)
ATTN_ROWS = 512
PACK_VMEM = 8 << 20
LAYER_VMEM = 20 << 20
F32 = jnp.float32
BF16 = jnp.bfloat16


def xor_pairs(size, step):
    return [(i, i ^ step) for i in range(size)]


def exchange(value, axis, size, step):
    return lax.ppermute(value, axis, xor_pairs(size, step))


def plan_chunks(layers, cols):
    pairs = [(layer, first) for layer in range(layers) for first in range(0, cols, LANES)]
    tail = [n for n in TAIL_PAIRS if len(pairs) >= 2 * sum(TAIL_PAIRS)] or [1]
    cuts = [0, len(pairs) - sum(tail)]
    for n in tail:
        cuts.append(cuts[-1] + n)
    chunks = []
    for low, high in zip(cuts[:-1], cuts[1:]):
        chunk = []
        for layer, first in pairs[low:high]:
            if chunk and chunk[-1][0] == layer:
                chunk[-1] = (layer, chunk[-1][1], chunk[-1][2] + LANES)
            else:
                chunk.append((layer, first, LANES))
        chunks.append(chunk)
    return chunks


def chunk_width(chunk):
    return sum(width for _, _, width in chunk)


def in_hbm(arrays):
    return [pltpu.with_memory_space_constraint(a, pltpu.HBM) for a in arrays]


def pack_chunk(chunk, arrays, seq_size):
    width = chunk_width(chunk)
    rows = [a.shape[2] for a in arrays]
    cols = arrays[0].shape[3] // seq_size

    def kernel(q_ref, g_ref, k_ref, v_ref, *rest):
        outs, sems = rest[:seq_size], rest[seq_size]
        me = lax.axis_index("seq")
        copies = []
        for j in list(range(1, seq_size)) + [0]:
            left = 0
            for n, (layer, first, part) in enumerate(chunk):
                start = pl.multiple_of((me ^ j) * cols + first, LANES)
                base = 0
                for i, ref in enumerate((q_ref, g_ref, k_ref, v_ref)):
                    copies.append(
                        pltpu.make_async_copy(
                            ref.at[layer, 0, :, pl.ds(start, part)],
                            outs[j].at[pl.ds(base, rows[i]), pl.ds(left, part)],
                            sems.at[j, n, i],
                        )
                    )
                    base += rows[i]
                left += part
        for c in copies:
            c.start()
        for c in copies:
            c.wait()

    return pl.pallas_call(
        kernel,
        out_shape=[jax.ShapeDtypeStruct((sum(rows), width), BF16)] * seq_size,
        in_specs=[pl.BlockSpec(memory_space=pltpu.HBM)] * 4,
        out_specs=[pl.BlockSpec(memory_space=pltpu.VMEM)] * seq_size,
        scratch_shapes=[pltpu.SemaphoreType.DMA((seq_size, len(chunk), 4))],
        compiler_params=pltpu.CompilerParams(vmem_limit_bytes=PACK_VMEM),
    )(*in_hbm(arrays))


def attention_into(bufs, dec, enc, kv_ref):
    cols = bufs[0].shape[1]
    count = len(bufs)
    per = LANES // HEAD_DIM
    group = max(1, ATTN_ROWS // dec)
    lane_head = lax.broadcasted_iota(jnp.int32, (1, LANES), 1) // HEAD_DIM
    rows = enc * count

    def stacked(base, ls):
        whole = jnp.concatenate([b[base : base + enc, ls].astype(F32) for b in bufs], axis=0)
        parts = [jnp.where(lane_head == h, whole, 0.0) for h in range(per)]
        return jnp.concatenate(parts, axis=0).astype(BF16)

    def chosen(stack):
        out = stack[:rows]
        for h in range(1, per):
            out = jnp.where(lane_head == h, stack[h * rows : (h + 1) * rows], out)
        return out.astype(BF16)

    nt = (((1,), (1,)), ((), ()))
    nn = (((1,), (0,)), ((), ()))
    for p in range(cols // LANES):
        ls = slice(p * LANES, (p + 1) * LANES)
        keys = stacked(2 * dec, ls)
        values = stacked(2 * dec + enc, ls)
        key_sum = value_sum = None
        for first in range(0, count, group):
            some = bufs[first : first + group]
            q = jnp.concatenate([b[0:dec, ls] for b in some], axis=0)
            g = jnp.concatenate([b[dec : 2 * dec, ls] for b in some], axis=0)
            width = q.shape[0]
            s = lax.dot_general(keys, q, nt, preferred_element_type=F32).reshape(per, rows, width)
            d = lax.dot_general(values, g, nt, preferred_element_type=F32).reshape(per, rows, width)
            e = jnp.exp(s - jnp.max(s, axis=1, keepdims=True))
            w = e * (1.0 / jnp.sum(e, axis=1, keepdims=True))
            delta = jnp.sum(w * d, axis=1, keepdims=True)
            ds = (w * (d - delta)).astype(BF16).reshape(per * rows, width)
            wl = w.astype(BF16).reshape(per * rows, width)
            vg = lax.dot_general(wl, g, nn, preferred_element_type=F32)
            kg = lax.dot_general(ds, q, nn, preferred_element_type=F32)
            key_sum = kg if key_sum is None else key_sum + kg
            value_sum = vg if value_sum is None else value_sum + vg
        kv_ref[:, ls] = chosen(key_sum)
        kv_ref[:, cols + p * LANES : cols + (p + 1) * LANES] = chosen(value_sum)


def weight_copies(chunk, key_weight, value_weight, dest, sems):
    copies = []
    left = 0
    for n, (layer, first, part) in enumerate(chunk):
        for i, src in enumerate((key_weight, value_weight)):
            copies.append(
                pltpu.make_async_copy(
                    src.at[layer, :, pl.ds(first, part)],
                    dest.at[:, pl.ds(i * chunk_width(chunk) + left, part)],
                    sems.at[n, i],
                )
            )
        left += part
    return copies


def load_weights(chunks, key_weight, value_weight, after):
    width = key_weight.shape[1]

    def kernel(kw, vw, after_ref, *rest):
        outs, sems = rest[: len(chunks)], rest[len(chunks) :]
        copies = []
        for chunk, out, sem in zip(chunks, outs, sems):
            copies += weight_copies(chunk, kw, vw, out, sem)
        for c in copies:
            c.start()
        for c in copies:
            c.wait()

    return pl.pallas_call(
        kernel,
        out_shape=[jax.ShapeDtypeStruct((width, 2 * chunk_width(c)), BF16) for c in chunks],
        in_specs=[pl.BlockSpec(memory_space=pltpu.HBM)] * 2 + [pl.BlockSpec(memory_space=pl.ANY)],
        out_specs=[pl.BlockSpec(memory_space=pltpu.VMEM)] * len(chunks),
        scratch_shapes=[pltpu.SemaphoreType.DMA((len(c), 2)) for c in chunks],
        compiler_params=pltpu.CompilerParams(vmem_limit_bytes=PACK_VMEM),
        name="load_weights",
    )(*in_hbm([key_weight, value_weight]), after)


def chunk_terms(bufs, weight, prior, dec, enc, last):
    count = len(bufs)
    width = weight.shape[0]
    rows = enc * count

    def kernel(*refs):
        buf_refs, w_ref, kv_ref = refs[:count], refs[count], refs[-1]
        prior_ref = None if prior is None else refs[count + 1]
        outs = refs[count + 1 + (prior is not None) : -1]
        attention_into(buf_refs, dec, enc, kv_ref)
        nt = (((1,), (1,)), ((), ()))
        for b in range(width // PROJ_BLOCK):
            bs = slice(b * PROJ_BLOCK, (b + 1) * PROJ_BLOCK)
            acc = lax.dot_general(kv_ref[...], w_ref[bs, :], nt, preferred_element_type=F32)
            if prior is not None:
                acc += prior_ref[:, bs]
            if last:
                for j in range(count):
                    outs[j][:, bs] = acc[j * enc : (j + 1) * enc].astype(outs[j].dtype)
            else:
                outs[0][:, bs] = acc

    if last:
        out_shape = [jax.ShapeDtypeStruct((enc, width), F32 if j == 0 else BF16) for j in range(count)]
    else:
        out_shape = [jax.ShapeDtypeStruct((rows, width), F32)]
    vmem = pl.BlockSpec(memory_space=pltpu.VMEM)
    operands = list(bufs) + [weight] + ([] if prior is None else [prior])
    return pl.pallas_call(
        kernel,
        out_shape=out_shape,
        in_specs=[vmem] * len(operands),
        out_specs=[vmem] * len(out_shape),
        scratch_shapes=[pltpu.VMEM((rows, weight.shape[1]), BF16)],
        compiler_params=pltpu.CompilerParams(vmem_limit_bytes=LAYER_VMEM),
    )(*operands)


def gather_rows(enc_final, seq_size):
    enc, width = enc_final.shape[1], enc_final.shape[2]
    rows = {0: [(enc_final, 0, 0, width)]}
    if seq_size == 4:
        half = 9 * width // 16 // LANES * LANES
        near = {j: exchange(enc_final, "seq", seq_size, j) for j in (1, 2)}
        for j in (1, 2):
            rows[j] = [(near[j], 0, 0, width)]
        sends = [near[1][:, :, :half], near[2][:, :, half:]]
        low = exchange(sends[0], "seq", seq_size, 2)
        high = exchange(sends[1], "seq", seq_size, 1)
        rows[3] = [(low, 0, 0, half), (high, 0, half, width - half)]
        return rows
    have, order = [enc_final], [0]
    step = 1
    while step < seq_size:
        whole = jnp.concatenate(have, axis=1) if len(have) > 1 else have[0]
        got = exchange(whole, "seq", seq_size, step)
        for place, j in enumerate(order):
            rows[j ^ step] = [(got, place * enc, 0, width)]
        have, order = have + [got], order + [j ^ step for j in order]
        step *= 2
    return rows


def gain_terms(pieces, rows):
    count = len(pieces)
    enc, width = pieces[0].shape
    arrays = []
    places = []
    for j in range(count):
        spots = []
        for array, base, first, cols in rows[j]:
            known = [n for n, a in enumerate(arrays) if a is array]
            if not known:
                arrays.append(array)
                known = [len(arrays) - 1]
            spots.append((known[0], base, first, cols))
        places.append(spots)
    cuts = sorted({first for spots in places for _, _, first, _ in spots} | {width})

    def kernel(*refs):
        piece_refs, row_refs, out_ref = refs[:count], refs[count:-1], refs[-1]
        inv = []
        for spots in places:
            square = 0.0
            for n, base, _, cols in spots:
                x = row_refs[n][0, pl.ds(base, enc), :].astype(F32)
                square = square + jnp.sum(x * x, axis=-1, keepdims=True)
            inv.append(lax.rsqrt(square * (1.0 / width) + 1e-06))
        for low, high in zip(cuts[:-1], cuts[1:]):
            terms = None
            for j, spots in enumerate(places):
                for n, base, first, cols in spots:
                    if first <= low and high <= first + cols:
                        x = row_refs[n][0, pl.ds(base, enc), pl.ds(low - first, high - low)]
                        product = piece_refs[j][:, low:high].astype(F32) * (x.astype(F32) * inv[j])
                        terms = product if terms is None else terms + product
            out_ref[:, low:high] = jnp.sum(terms, axis=0, keepdims=True)

    return pl.pallas_call(
        kernel,
        out_shape=jax.ShapeDtypeStruct((1, width), F32),
        compiler_params=pltpu.CompilerParams(vmem_limit_bytes=PACK_VMEM),
        name="gain_terms",
    )(*pieces, *arrays)


def finish(own, received, enc_final, norm_gain):
    enc, width = own.shape

    def kernel(own_ref, *refs):
        recv_refs = refs[: len(received)]
        final_ref, gain_ref, grad_ref = refs[len(received) :]
        state = own_ref[...]
        for r in recv_refs:
            state = state + r[...].astype(F32)
        final = final_ref[0].astype(F32)
        inv_rms = lax.rsqrt(jnp.mean(final * final, axis=-1, keepdims=True) + 1e-06)
        normed = final * inv_rms
        scaled = gain_ref[...] * state
        mean = jnp.mean(scaled * normed, axis=-1, keepdims=True)
        grad_ref[0] = (inv_rms * (scaled - normed * mean)).astype(BF16)

    return pl.pallas_call(
        kernel,
        out_shape=jax.ShapeDtypeStruct((1, enc, width), BF16),
        compiler_params=pltpu.CompilerParams(vmem_limit_bytes=PACK_VMEM),
        name="finish",
    )(own, *received, enc_final, norm_gain.reshape(1, width))


def peer_steps(docs, seq_size):
    steps = [1 << b for b in range(seq_size.bit_length() - 1)]
    if docs % 2:
        return [(step, 0) for step in steps]
    return [(steps[n], steps[n + 1] if n + 1 < len(steps) else 0) for n in range(0, len(steps), 2)]


def add_peers(value, docs, seq_size, low, high):
    if not high:
        return value + exchange(value, "seq", seq_size, low)
    spots = [(d, s) for d in range(docs) for s in range(seq_size)]
    one = [(d * seq_size + s, d * seq_size + (s ^ (low if d % 2 else low ^ high))) for d, s in spots]
    two = [(d * seq_size + s, d * seq_size + (s ^ high)) for d, s in spots if d % 2]
    first = lax.ppermute(value, ("dp", "seq"), one)
    second = lax.ppermute(value, ("dp", "seq"), two)
    own = jnp.where(lax.axis_index("dp") % 2 == 0, value, 0.0)
    part = (first + second) + own
    return part + exchange(part, "dp", docs, 1)


def body(
    enc_final, norm_gain, dec_queries, out_grad, enc_keys, enc_values, key_weight, value_weight
):
    seq = lax.axis_size("seq")
    docs = lax.axis_size("dp")
    layers = dec_queries.shape[0]
    dec, enc = dec_queries.shape[2], enc_keys.shape[2]
    arrays = (dec_queries, out_grad, enc_keys, enc_values)
    chunks = plan_chunks(layers, key_weight.shape[2])
    rows = gather_rows(enc_final, seq)
    gathered = []
    for chunk in chunks:
        bufs = pack_chunk(chunk, arrays, seq)
        moved = [bufs[0]]
        for j in range(1, seq):
            moved.append(exchange(bufs[j], "seq", seq, j))
        gathered.append(moved)
    weights = load_weights(chunks, key_weight, value_weight, gathered[-1][0])
    prior = None
    for index in range(len(chunks)):
        outs = chunk_terms(gathered[index], weights[index], prior, dec, enc, index == len(chunks) - 1)
        prior = outs[0]
    received = [exchange(outs[j], "seq", seq, j) for j in range(1, seq)]
    gain = gain_terms(outs, rows)
    enc_grad = finish(outs[0], received, enc_final, norm_gain)
    for b in range(docs.bit_length() - 1):
        gain = gain + exchange(gain, "dp", docs, 1 << b)
    for low, high in peer_steps(docs, seq):
        gain = add_peers(gain, docs, seq, low, high)
    return (enc_grad, gain[0] / docs)


def solution(mesh):
    placed = (
        P("dp", "seq", None),
        P(),
        P(None, "dp", "seq", None),
        P(None, "dp", "seq", None),
        P(None, "dp", "seq", None),
        P(None, "dp", "seq", None),
        P(None, None, "seq"),
        P(None, None, "seq"),
    )

    def whole(*args):
        step = jax.shard_map(body, mesh=mesh, in_specs=placed, out_specs=(P("dp", "seq", None), P()), check_vma=False)
        return step(*args)

    return whole
```

```python
import jax
import jax.numpy as jnp
from jax import lax
from jax.experimental import pallas as pl
from jax.experimental.pallas import tpu as pltpu
from jax.sharding import PartitionSpec as P


HEAD_DIM = 64
LANES = 128
PROJ_BLOCK = 2048
TAIL_PAIRS = (2, 1)
ATTN_ROWS = 512
PACK_VMEM = 8 << 20
LAYER_VMEM = 20 << 20
F32 = jnp.float32
BF16 = jnp.bfloat16


def xor_pairs(size, step):
    return [(i, i ^ step) for i in range(size)]


def exchange(value, axis, size, step):
    return lax.ppermute(value, axis, xor_pairs(size, step))


def plan_chunks(layers, cols):
    pairs = [(layer, first) for layer in range(layers) for first in range(0, cols, LANES)]
    tail = [n for n in TAIL_PAIRS if len(pairs) >= 2 * sum(TAIL_PAIRS)] or [1]
    cuts = [0, len(pairs) - sum(tail)]
    for n in tail:
        cuts.append(cuts[-1] + n)
    chunks = []
    for low, high in zip(cuts[:-1], cuts[1:]):
        chunk = []
        for layer, first in pairs[low:high]:
            if chunk and chunk[-1][0] == layer:
                chunk[-1] = (layer, chunk[-1][1], chunk[-1][2] + LANES)
            else:
                chunk.append((layer, first, LANES))
        chunks.append(chunk)
    return chunks


def chunk_width(chunk):
    return sum(width for _, _, width in chunk)


def in_hbm(arrays):
    return [pltpu.with_memory_space_constraint(a, pltpu.HBM) for a in arrays]


def pack_chunk(chunk, arrays, seq_size):
    width = chunk_width(chunk)
    rows = [a.shape[2] for a in arrays]
    cols = arrays[0].shape[3] // seq_size

    def kernel(q_ref, g_ref, k_ref, v_ref, *rest):
        outs, sems = rest[:seq_size], rest[seq_size]
        me = lax.axis_index("seq")
        copies = []
        for j in list(range(1, seq_size)) + [0]:
            left = 0
            for n, (layer, first, part) in enumerate(chunk):
                start = pl.multiple_of((me ^ j) * cols + first, LANES)
                base = 0
                for i, ref in enumerate((q_ref, g_ref, k_ref, v_ref)):
                    copies.append(
                        pltpu.make_async_copy(
                            ref.at[layer, 0, :, pl.ds(start, part)],
                            outs[j].at[pl.ds(base, rows[i]), pl.ds(left, part)],
                            sems.at[j, n, i],
                        )
                    )
                    base += rows[i]
                left += part
        for c in copies:
            c.start()
        for c in copies:
            c.wait()

    return pl.pallas_call(
        kernel,
        out_shape=[jax.ShapeDtypeStruct((sum(rows), width), BF16)] * seq_size,
        in_specs=[pl.BlockSpec(memory_space=pltpu.HBM)] * 4,
        out_specs=[pl.BlockSpec(memory_space=pltpu.VMEM)] * seq_size,
        scratch_shapes=[pltpu.SemaphoreType.DMA((seq_size, len(chunk), 4))],
        compiler_params=pltpu.CompilerParams(vmem_limit_bytes=PACK_VMEM),
    )(*in_hbm(arrays))


def attention_into(bufs, dec, enc, kv_ref):
    cols = bufs[0].shape[1]
    count = len(bufs)
    per = LANES // HEAD_DIM
    group = max(1, ATTN_ROWS // dec)
    lane_head = lax.broadcasted_iota(jnp.int32, (1, LANES), 1) // HEAD_DIM
    rows = enc * count

    def stacked(base, ls):
        whole = jnp.concatenate([b[base : base + enc, ls].astype(F32) for b in bufs], axis=0)
        parts = [jnp.where(lane_head == h, whole, 0.0) for h in range(per)]
        return jnp.concatenate(parts, axis=0).astype(BF16)

    def chosen(stack):
        out = stack[:rows]
        for h in range(1, per):
            out = jnp.where(lane_head == h, stack[h * rows : (h + 1) * rows], out)
        return out.astype(BF16)

    nt = (((1,), (1,)), ((), ()))
    nn = (((1,), (0,)), ((), ()))
    for p in range(cols // LANES):
        ls = slice(p * LANES, (p + 1) * LANES)
        keys = stacked(2 * dec, ls)
        values = stacked(2 * dec + enc, ls)
        key_sum = value_sum = None
        for first in range(0, count, group):
            some = bufs[first : first + group]
            q = jnp.concatenate([b[0:dec, ls] for b in some], axis=0)
            g = jnp.concatenate([b[dec : 2 * dec, ls] for b in some], axis=0)
            width = q.shape[0]
            s = lax.dot_general(keys, q, nt, preferred_element_type=F32).reshape(per, rows, width)
            d = lax.dot_general(values, g, nt, preferred_element_type=F32).reshape(per, rows, width)
            e = jnp.exp(s - jnp.max(s, axis=1, keepdims=True))
            w = e * (1.0 / jnp.sum(e, axis=1, keepdims=True))
            delta = jnp.sum(w * d, axis=1, keepdims=True)
            ds = (w * (d - delta)).astype(BF16).reshape(per * rows, width)
            wl = w.astype(BF16).reshape(per * rows, width)
            vg = lax.dot_general(wl, g, nn, preferred_element_type=F32)
            kg = lax.dot_general(ds, q, nn, preferred_element_type=F32)
            key_sum = kg if key_sum is None else key_sum + kg
            value_sum = vg if value_sum is None else value_sum + vg
        kv_ref[:, ls] = chosen(key_sum)
        kv_ref[:, cols + p * LANES : cols + (p + 1) * LANES] = chosen(value_sum)


def weight_copies(chunk, key_weight, value_weight, dest, sems):
    copies = []
    left = 0
    for n, (layer, first, part) in enumerate(chunk):
        for i, src in enumerate((key_weight, value_weight)):
            copies.append(
                pltpu.make_async_copy(
                    src.at[layer, :, pl.ds(first, part)],
                    dest.at[:, pl.ds(i * chunk_width(chunk) + left, part)],
                    sems.at[n, i],
                )
            )
        left += part
    return copies


def load_weights(chunks, key_weight, value_weight, after):
    width = key_weight.shape[1]

    def kernel(kw, vw, after_ref, *rest):
        outs, sems = rest[: len(chunks)], rest[len(chunks) :]
        copies = []
        for chunk, out, sem in zip(chunks, outs, sems):
            copies += weight_copies(chunk, kw, vw, out, sem)
        for c in copies:
            c.start()
        for c in copies:
            c.wait()

    return pl.pallas_call(
        kernel,
        out_shape=[jax.ShapeDtypeStruct((width, 2 * chunk_width(c)), BF16) for c in chunks],
        in_specs=[pl.BlockSpec(memory_space=pltpu.HBM)] * 2 + [pl.BlockSpec(memory_space=pl.ANY)],
        out_specs=[pl.BlockSpec(memory_space=pltpu.VMEM)] * len(chunks),
        scratch_shapes=[pltpu.SemaphoreType.DMA((len(c), 2)) for c in chunks],
        compiler_params=pltpu.CompilerParams(vmem_limit_bytes=PACK_VMEM),
        name="load_weights",
    )(*in_hbm([key_weight, value_weight]), after)


def chunk_terms(bufs, weight, prior, dec, enc, last):
    count = len(bufs)
    width = weight.shape[0]
    rows = enc * count

    def kernel(*refs):
        buf_refs, w_ref, kv_ref = refs[:count], refs[count], refs[-1]
        prior_ref = None if prior is None else refs[count + 1]
        outs = refs[count + 1 + (prior is not None) : -1]
        attention_into(buf_refs, dec, enc, kv_ref)
        nt = (((1,), (1,)), ((), ()))
        for b in range(width // PROJ_BLOCK):
            bs = slice(b * PROJ_BLOCK, (b + 1) * PROJ_BLOCK)
            acc = lax.dot_general(kv_ref[...], w_ref[bs, :], nt, preferred_element_type=F32)
            if prior is not None:
                acc += prior_ref[:, bs]
            if last:
                for j in range(count):
                    outs[j][:, bs] = acc[j * enc : (j + 1) * enc].astype(outs[j].dtype)
            else:
                outs[0][:, bs] = acc

    if last:
        out_shape = [jax.ShapeDtypeStruct((enc, width), F32 if j == 0 else BF16) for j in range(count)]
    else:
        out_shape = [jax.ShapeDtypeStruct((rows, width), F32)]
    vmem = pl.BlockSpec(memory_space=pltpu.VMEM)
    operands = list(bufs) + [weight] + ([] if prior is None else [prior])
    return pl.pallas_call(
        kernel,
        out_shape=out_shape,
        in_specs=[vmem] * len(operands),
        out_specs=[vmem] * len(out_shape),
        scratch_shapes=[pltpu.VMEM((rows, weight.shape[1]), BF16)],
        compiler_params=pltpu.CompilerParams(vmem_limit_bytes=LAYER_VMEM),
    )(*operands)


def gather_rows(enc_final, seq_size):
    enc, width = enc_final.shape[1], enc_final.shape[2]
    rows = {0: [(enc_final, 0, 0, width)]}
    if seq_size == 4:
        half = 9 * width // 16 // LANES * LANES
        near = {j: exchange(enc_final, "seq", seq_size, j) for j in (1, 2)}
        for j in (1, 2):
            rows[j] = [(near[j], 0, 0, width)]
        sends = [near[1][:, :, :half], near[2][:, :, half:]]
        low = exchange(sends[0], "seq", seq_size, 2)
        high = exchange(sends[1], "seq", seq_size, 1)
        rows[3] = [(low, 0, 0, half), (high, 0, half, width - half)]
        return rows
    have, order = [enc_final], [0]
    step = 1
    while step < seq_size:
        whole = jnp.concatenate(have, axis=1) if len(have) > 1 else have[0]
        got = exchange(whole, "seq", seq_size, step)
        for place, j in enumerate(order):
            rows[j ^ step] = [(got, place * enc, 0, width)]
        have, order = have + [got], order + [j ^ step for j in order]
        step *= 2
    return rows


def row_scales(rows):
    whole = [j for j in sorted(rows) if len(rows[j]) == 1]
    enc = rows[0][0][0].shape[1]

    def kernel(*refs):
        for n, j in enumerate(whole):
            _, base, _, cols = rows[j][0]
            x = refs[n][0, pl.ds(base, enc), :].astype(F32)
            total = jnp.sum(x * x, axis=-1, keepdims=True)
            scale = lax.rsqrt(total * (1.0 / cols) + 1e-06)
            refs[-1][pl.ds(n * enc, enc), :] = jnp.broadcast_to(scale, (enc, LANES))

    scales = pl.pallas_call(
        kernel,
        out_shape=jax.ShapeDtypeStruct((len(whole) * enc, LANES), F32),
        compiler_params=pltpu.CompilerParams(vmem_limit_bytes=PACK_VMEM),
        name="row_scales",
    )(*[rows[j][0][0] for j in whole])
    return whole, scales


def gain_terms(pieces, rows, whole, scales):
    count = len(pieces)
    enc, width = pieces[0].shape
    arrays = []
    places = []
    for j in range(count):
        spots = []
        for array, base, first, cols in rows[j]:
            known = [n for n, a in enumerate(arrays) if a is array]
            if not known:
                arrays.append(array)
                known = [len(arrays) - 1]
            spots.append((known[0], base, first, cols))
        places.append(spots)
    cuts = sorted({first for spots in places for _, _, first, _ in spots} | {width})

    def kernel(*refs):
        piece_refs, row_refs, scale_ref, out_ref = refs[:count], refs[count:-2], refs[-2], refs[-1]
        inv = []
        for j, spots in enumerate(places):
            if j in whole:
                inv.append(scale_ref[pl.ds(whole.index(j) * enc, enc), 0:1])
                continue
            square = 0.0
            for n, base, _, cols in spots:
                x = row_refs[n][0, pl.ds(base, enc), :].astype(F32)
                square = square + jnp.sum(x * x, axis=-1, keepdims=True)
            inv.append(lax.rsqrt(square * (1.0 / width) + 1e-06))
        for low, high in zip(cuts[:-1], cuts[1:]):
            terms = None
            for j, spots in enumerate(places):
                for n, base, first, cols in spots:
                    if first <= low and high <= first + cols:
                        x = row_refs[n][0, pl.ds(base, enc), pl.ds(low - first, high - low)]
                        product = piece_refs[j][:, low:high].astype(F32) * (x.astype(F32) * inv[j])
                        terms = product if terms is None else terms + product
            out_ref[:, low:high] = jnp.sum(terms, axis=0, keepdims=True)

    return pl.pallas_call(
        kernel,
        out_shape=jax.ShapeDtypeStruct((1, width), F32),
        compiler_params=pltpu.CompilerParams(vmem_limit_bytes=PACK_VMEM),
        name="gain_terms",
    )(*pieces, *arrays, scales)


def finish(own, received, enc_final, norm_gain):
    enc, width = own.shape

    def kernel(own_ref, *refs):
        recv_refs = refs[: len(received)]
        final_ref, gain_ref, grad_ref = refs[len(received) :]
        state = own_ref[...]
        for r in recv_refs:
            state = state + r[...].astype(F32)
        final = final_ref[0].astype(F32)
        inv_rms = lax.rsqrt(jnp.mean(final * final, axis=-1, keepdims=True) + 1e-06)
        normed = final * inv_rms
        scaled = gain_ref[...] * state
        mean = jnp.mean(scaled * normed, axis=-1, keepdims=True)
        grad_ref[0] = (inv_rms * (scaled - normed * mean)).astype(BF16)

    return pl.pallas_call(
        kernel,
        out_shape=jax.ShapeDtypeStruct((1, enc, width), BF16),
        compiler_params=pltpu.CompilerParams(vmem_limit_bytes=PACK_VMEM),
        name="finish",
    )(own, *received, enc_final, norm_gain.reshape(1, width))


def peer_steps(docs, seq_size):
    steps = [1 << b for b in range(seq_size.bit_length() - 1)]
    if docs % 2:
        return [(step, 0) for step in steps]
    return [(steps[n], steps[n + 1] if n + 1 < len(steps) else 0) for n in range(0, len(steps), 2)]


def add_peers(value, docs, seq_size, low, high):
    if not high:
        return value + exchange(value, "seq", seq_size, low)
    spots = [(d, s) for d in range(docs) for s in range(seq_size)]
    one = [(d * seq_size + s, d * seq_size + (s ^ (low if d % 2 else low ^ high))) for d, s in spots]
    two = [(d * seq_size + s, d * seq_size + (s ^ high)) for d, s in spots if d % 2]
    first = lax.ppermute(value, ("dp", "seq"), one)
    second = lax.ppermute(value, ("dp", "seq"), two)
    own = jnp.where(lax.axis_index("dp") % 2 == 0, value, 0.0)
    part = (first + second) + own
    return part + exchange(part, "dp", docs, 1)


def body(
    enc_final, norm_gain, dec_queries, out_grad, enc_keys, enc_values, key_weight, value_weight
):
    seq = lax.axis_size("seq")
    docs = lax.axis_size("dp")
    layers = dec_queries.shape[0]
    dec, enc = dec_queries.shape[2], enc_keys.shape[2]
    arrays = (dec_queries, out_grad, enc_keys, enc_values)
    chunks = plan_chunks(layers, key_weight.shape[2])
    rows = gather_rows(enc_final, seq)
    gathered = []
    for chunk in chunks:
        bufs = pack_chunk(chunk, arrays, seq)
        moved = [bufs[0]]
        for j in range(1, seq):
            moved.append(exchange(bufs[j], "seq", seq, j))
        gathered.append(moved)
    weights = load_weights(chunks, key_weight, value_weight, gathered[-1][0])
    prior = None
    for index in range(len(chunks)):
        outs = chunk_terms(gathered[index], weights[index], prior, dec, enc, index == len(chunks) - 1)
        prior = outs[0]
    received = [exchange(outs[j], "seq", seq, j) for j in range(1, seq)]
    whole, scales = row_scales(rows)
    gain = gain_terms(outs, rows, whole, scales)
    enc_grad = finish(outs[0], received, enc_final, norm_gain)
    for b in range(docs.bit_length() - 1):
        gain = gain + exchange(gain, "dp", docs, 1 << b)
    for low, high in peer_steps(docs, seq):
        gain = add_peers(gain, docs, seq, low, high)
    return (enc_grad, gain[0] / docs)


def solution(mesh):
    placed = (
        P("dp", "seq", None),
        P(),
        P(None, "dp", "seq", None),
        P(None, "dp", "seq", None),
        P(None, "dp", "seq", None),
        P(None, "dp", "seq", None),
        P(None, None, "seq"),
        P(None, None, "seq"),
    )

    def whole(*args):
        step = jax.shard_map(body, mesh=mesh, in_specs=placed, out_specs=(P("dp", "seq", None), P()), check_vma=False)
        return step(*args)

    return whole
```
